256 devices in a mesh: az: 64 (over x, y_hi, z), ax: 4 (over y_lo, core).
Axes of the slice: x: 4, y: 4 (y_hi: 2, y_lo: 2; y = y_hi * 2 + y_lo), z: 8, core: 2. Of those that a mesh axis runs over, the one named last changes fastest.
Arguments:
- fields: float32 [5, 64, 1024, 512], P(None, 'ax', 'az'), may hold values from -6.5 to 6.5, as said below
Outputs:
- advanced: float32 [5, 64, 1024, 512], P(None, 'ax', 'az')
The draws below stay inside these ranges and needn't reach their ends.
Inputs may be any that keep to these rules, and one draw needn't show every extreme that they name: `fields`: each field is a rough part plus, on every axial plane and cycle, a constant and a first azimuthal harmonic.
All inputs are finite; a program needn't handle non-finite values.
Results may differ from the reference program's by a relative error of at most 0.0003.
Values sent between devices are 32-bit elements; how exact they have to be, the bound alone decides.
A program may use at most 128 MiB of HBM per device.

```python
import jax
import jax.numpy as jnp
from jax import lax

NR = 512
NEAR = 40
NT = 1024
NZ = 64
MODES = 128


def draw_fields(key, part):
    shape = (5, NZ, NT, NR)
    small_shape = (5, NZ, 1, NR)
    rough_key = jax.random.fold_in(key, 11)
    height_key = jax.random.fold_in(key, 12)
    phase_key = jax.random.fold_in(key, 13)
    level_key = jax.random.fold_in(key, 14)
    theta = jnp.arange(NT, dtype=jnp.float32) * (2.0 * jnp.pi / NT)
    rough = jnp.clip(jax.random.normal(rough_key, shape, jnp.float32), -4.0, 4.0)
    height = jax.random.uniform(height_key, small_shape, jnp.float32, 0.3, 1.2)
    level = jax.random.uniform(level_key, small_shape, jnp.float32, -0.6, 0.6)
    phase = jax.random.uniform(phase_key, small_shape, jnp.float32, -jnp.pi, jnp.pi)
    return rough + height * jnp.cos(theta[None, None, :, None] + phase) + level


def setup_inputs(seed: int = 0) -> dict:
    keys = jax.random.split(jax.random.key(seed), 2)
    fields = draw_fields(jax.random.fold_in(keys[1], 71), 0)
    return {"fields": fields}


viscosity = 0.2
time_step = 0.1
buoyancy = 1.0


def mode_tables(theta_index, total_theta, modes):
    column = jnp.arange(modes, dtype=jnp.int32)
    product = (theta_index[:, None] * column[None, :]) % total_theta
    angle = product.astype(jnp.float32) * (2.0 * jnp.pi / total_theta)
    cosine = jnp.cos(angle)
    sine = jnp.sin(angle)
    weight = jnp.where(column == 0, 1.0, 2.0).astype(jnp.float32) / total_theta
    forward = jnp.concatenate([cosine * weight[None, :], sine * (2.0 / total_theta)], axis=1)
    inverse = jnp.concatenate([cosine, sine], axis=1)
    return forward, inverse


def cycle_mask(cycles, modes):
    cycle_index = jnp.arange(cycles, dtype=jnp.int32)
    cutoff = jnp.minimum((355 * (2 * cycle_index + 1)) // 226, modes - 1)
    column = jnp.arange(modes, dtype=jnp.int32)
    keep = (column[None, :] <= cutoff[:, None]).astype(jnp.float32)
    return jnp.concatenate([keep, keep], axis=1)


def operators(center, radial_plus, radial_minus, theta_plus, theta_minus, axial_plus, axial_minus, total_theta):
    radius = jnp.arange(center.shape[-1], dtype=jnp.float32) + 0.5
    step_angle = 2.0 * jnp.pi / total_theta
    d_radial = (radial_plus - radial_minus) * 0.5
    d_theta = (theta_plus - theta_minus) / (2.0 * step_angle)
    d_axial = (axial_plus - axial_minus) * 0.5
    laplace = radial_plus - 2.0 * center + radial_minus + (radial_plus - radial_minus) / (2.0 * radius)
    laplace = laplace + (theta_plus - 2.0 * center + theta_minus) / (radius * radius * step_angle * step_angle)
    laplace = laplace + axial_plus - 2.0 * center + axial_minus
    return d_radial, d_theta, d_axial, laplace


def reference(fields):
    theta_index = jnp.arange(NT, dtype=jnp.int32)
    forward, inverse = mode_tables(theta_index, NT, MODES)
    inner_cycles = fields[:, :, :, :NEAR]
    spectra = jnp.einsum("fztj,tc->fzjc", inner_cycles, forward, precision=lax.Precision.HIGHEST)
    kept = spectra * cycle_mask(NEAR, MODES)[None, None]
    smoothed = jnp.einsum("fzjc,tc->fztj", kept, inverse, precision=lax.Precision.HIGHEST)
    state = jnp.concatenate([smoothed, fields[:, :, :, NEAR:]], axis=3)
    flip = jnp.array([-1.0, -1.0, 1.0, 1.0, 1.0], dtype=jnp.float32)
    opposite = jnp.roll(state[:, :, :, 0], NT // 2, axis=2) * flip[:, None, None]
    radius = jnp.arange(NR, dtype=jnp.float32) + 0.5
    radial_u = state[0]
    theta_u = state[1]
    axial_u = state[2]
    results = []
    theta_grads = []
    for index in range(5):
        field = state[index]
        radial_plus = jnp.concatenate([field[:, :, 1:], jnp.zeros_like(field[:, :, :1])], axis=2)
        radial_minus = jnp.concatenate([opposite[index][:, :, None], field[:, :, :-1]], axis=2)
        theta_plus = jnp.roll(field, -1, axis=1)
        theta_minus = jnp.roll(field, 1, axis=1)
        zero_plane = jnp.zeros_like(field[:1])
        axial_plus = jnp.concatenate([field[1:], zero_plane], axis=0)
        axial_minus = jnp.concatenate([zero_plane, field[:-1]], axis=0)
        d_radial, d_theta, d_axial, laplace = operators(field, radial_plus, radial_minus, theta_plus, theta_minus, axial_plus, axial_minus, NT)
        change = -(radial_u * d_radial + theta_u / radius * d_theta + axial_u * d_axial) + viscosity * laplace
        results.append(change)
        if index < 2:
            theta_grads.append(d_theta)
    inverse_square = 1.0 / (radius * radius)
    results[0] = results[0] + theta_u * theta_u / radius - viscosity * (radial_u * inverse_square + 2.0 * inverse_square * theta_grads[1])
    results[1] = results[1] - radial_u * theta_u / radius - viscosity * (theta_u * inverse_square - 2.0 * inverse_square * theta_grads[0])
    results[2] = results[2] + buoyancy * state[3]
    return state + time_step * jnp.stack(results, axis=0)
```

```python
import functools

import jax
import jax.numpy as jnp
import ml_dtypes
import numpy as np
from jax import lax
from jax.experimental import pallas as pl
from jax.experimental.pallas import tpu as pltpu
from jax.sharding import PartitionSpec as P

NEAR = 40
FIELDS = 5
MODES = 128
LANES = 128
HALF = 64
QUARTER = 10
MESH = pl.DeviceIdType.MESH

viscosity = 0.2
time_step = 0.1
buoyancy = 1.0


def split(table, pieces):
    out = []
    rest = table.astype(np.float32)
    for _ in range(pieces):
        piece = rest.astype(ml_dtypes.bfloat16)
        out.append(piece)
        rest = rest - piece.astype(np.float32)
    return np.stack(out)


def transform_tables(sectors, theta_dev):
    total = sectors * theta_dev
    half = theta_dev // 2
    theta = (
        np.arange(sectors)[None, :, None] * theta_dev
        + np.arange(2)[:, None, None] * half
        + np.arange(half)[None, None, :]
    ).reshape(2, sectors * half)
    mode = np.arange(MODES)
    angle = (theta[:, :, None] * mode[None, None, :] % total) * (2.0 * np.pi / total)
    basis = np.concatenate([np.cos(angle), np.sin(angle)], axis=2)
    weight = np.concatenate([np.where(mode == 0, 1.0, 2.0), np.full(MODES, 2.0)]) / total
    forward = (basis * weight).transpose(0, 2, 1).reshape(4 * MODES, sectors * half)
    inverse = basis.transpose(1, 0, 2).reshape(sectors * half, 4 * MODES)
    return split(forward, 2), split(inverse, 3)


def filter_kernel(
    sectors,
    fields,
    forward_hbm,
    inverse_hbm,
    near,
    raw,
    forward,
    inverse,
    send1,
    recv1,
    send2,
    recv2,
    load_sem,
    send_sem1,
    recv_sem1,
    send_sem2,
    recv_sem2,
):
    me = lax.axis_index("az")
    planes = raw.shape[1]
    half = raw.shape[2] // 2
    load = pltpu.make_async_copy(fields.at[:, :, :, pl.ds(0, LANES)], raw, load_sem.at[0])
    load.start()
    load_forward = pltpu.make_async_copy(forward_hbm, forward, load_sem.at[1])
    load_forward.start()
    load_inverse = pltpu.make_async_copy(inverse_hbm, inverse, load_sem.at[2])
    load_inverse.start()
    barrier = pltpu.get_barrier_semaphore()

    def greet(i, carry):
        pl.semaphore_signal(
            barrier, inc=1, device_id={"az": (me + i) % sectors}, device_id_type=MESH
        )
        return carry

    lax.fori_loop(1, sectors, greet, 0)
    load.wait()
    lane = lax.broadcasted_iota(jnp.int32, (half, LANES), 1)

    def pack(k, carry):
        tail0 = raw[4, k, :half, :]
        tail1 = raw[4, k, half:, :]
        for f in range(4):
            shift = NEAR - QUARTER * f
            first = jnp.where(lane < NEAR, raw[f, k, :half, :], pltpu.roll(tail0, shift, 1))
            second = jnp.where(lane < NEAR, raw[f, k, half:, :], pltpu.roll(tail1, shift, 1))
            send1[k * 4 + f] = jnp.where(lane < HALF, first, pltpu.roll(second, HALF, 1))
        return carry

    lax.fori_loop(0, planes, pack, 0)
    pl.semaphore_wait(barrier, sectors - 1)

    def exchange(source, target, send_sem, recv_sem):
        def post(i, carry):
            peer = (me + i) % sectors
            pltpu.make_async_remote_copy(
                src_ref=source.at[peer],
                dst_ref=target.at[me],
                send_sem=send_sem,
                recv_sem=recv_sem,
                device_id={"az": peer},
                device_id_type=MESH,
            ).start()
            return carry

        lax.fori_loop(1, sectors, post, 0)
        target[me] = source[me]
        return pltpu.make_async_remote_copy(
            src_ref=source.at[pl.ds(0, sectors - 1)],
            dst_ref=target.at[pl.ds(0, sectors - 1)],
            send_sem=send_sem,
            recv_sem=recv_sem,
            device_id={"az": (me + 1) % sectors},
            device_id_type=MESH,
        )

    first = exchange(send1, recv1, send_sem1, recv_sem1)
    load_forward.wait()
    load_inverse.wait()
    first.wait_recv()
    values = recv1[...].reshape(sectors * half, LANES)
    high = values.astype(jnp.bfloat16)
    low = (values - high.astype(jnp.float32)).astype(jnp.bfloat16)
    dot = functools.partial(jnp.dot, preferred_element_type=jnp.float32)
    spectra = dot(forward[0], high) + (dot(forward[0], low) + dot(forward[1], high))
    row = lax.broadcasted_iota(jnp.int32, (2 * MODES, LANES), 0)
    column = lax.broadcasted_iota(jnp.int32, (2 * MODES, LANES), 1)
    spectra = jnp.where(column < HALF, spectra[: 2 * MODES], spectra[2 * MODES :])
    spectra = spectra + pltpu.roll(spectra, HALF, 1)
    slot = jnp.where(column < HALF, column, column - HALF)
    cycle = jnp.where(slot < NEAR, slot, slot - NEAR + QUARTER * (me % 4))
    cutoff = jnp.floor((355 * (2 * cycle + 1)).astype(jnp.float32) / 226.0 + 0.001)
    mode = jnp.where(row < MODES, row, row - MODES).astype(jnp.float32)
    spectra = jnp.where(mode <= jnp.minimum(cutoff, MODES - 1.0), spectra, 0.0)
    spectra = jnp.concatenate(
        [jnp.where(column < HALF, spectra, 0.0), jnp.where(column < HALF, 0.0, spectra)], axis=0
    )
    high = spectra.astype(jnp.bfloat16)
    rest = spectra - high.astype(jnp.float32)
    middle = rest.astype(jnp.bfloat16)
    low = (rest - middle.astype(jnp.float32)).astype(jnp.bfloat16)
    smooth = dot(inverse[0], low) + dot(inverse[1], middle) + dot(inverse[2], high)
    smooth = smooth + (dot(inverse[0], middle) + dot(inverse[1], high))
    smooth = smooth + dot(inverse[0], high)
    send2[...] = smooth.reshape(sectors, half, LANES)
    second = exchange(send2, recv2, send_sem2, recv_sem2)
    second.wait_recv()

    def unpack(k, carry):
        tail0 = raw[4, k, :half, :]
        tail1 = raw[4, k, half:, :]
        for f in range(4):
            got = recv2[k * 4 + f]
            near[f, k, :half, :] = jnp.where(lane < NEAR, got, raw[f, k, :half, :])
            near[f, k, half:, :] = jnp.where(
                lane < NEAR, pltpu.roll(got, HALF, 1), raw[f, k, half:, :]
            )
            here = (lane >= QUARTER * f) & (lane < QUARTER * (f + 1))
            shift = (QUARTER * f - NEAR) % LANES
            tail0 = jnp.where(here, pltpu.roll(got, shift, 1), tail0)
            tail1 = jnp.where(here, pltpu.roll(got, (shift + HALF) % LANES, 1), tail1)
        near[4, k, :half, :] = tail0
        near[4, k, half:, :] = tail1
        return carry

    lax.fori_loop(0, planes, unpack, 0)
    first.wait_send()
    second.wait_send()


def filtered(fields, sectors):
    count, planes, theta_dev, radial = fields.shape
    half = theta_dev // 2
    forward, inverse = transform_tables(sectors, theta_dev)
    any_spec = pl.BlockSpec(memory_space=pl.ANY)
    return pl.pallas_call(
        functools.partial(filter_kernel, sectors),
        out_shape=jax.ShapeDtypeStruct((count, planes, theta_dev, LANES), jnp.float32),
        in_specs=[any_spec, any_spec, any_spec],
        out_specs=pl.BlockSpec(memory_space=pltpu.VMEM),
        scratch_shapes=[
            pltpu.VMEM((count, planes, theta_dev, LANES), jnp.float32),
            pltpu.VMEM(forward.shape, jnp.bfloat16),
            pltpu.VMEM(inverse.shape, jnp.bfloat16),
            pltpu.VMEM((sectors, half, LANES), jnp.float32),
            pltpu.VMEM((sectors, half, LANES), jnp.float32),
            pltpu.VMEM((sectors, half, LANES), jnp.float32),
            pltpu.VMEM((sectors, half, LANES), jnp.float32),
            pltpu.SemaphoreType.DMA((3,)),
            pltpu.SemaphoreType.DMA,
            pltpu.SemaphoreType.DMA,
            pltpu.SemaphoreType.DMA,
            pltpu.SemaphoreType.DMA,
        ],
        compiler_params=pltpu.CompilerParams(
            collective_id=0, has_side_effects=True, vmem_limit_bytes=48 << 20
        ),
        name="azimuthal_filter",
    )(fields, jnp.asarray(forward), jnp.asarray(inverse))


def swapped(block, axis, distance):
    count = lax.axis_size(axis)
    route = []
    for low in range(count):
        high = low | 1 << distance
        if high != low and high < count:
            route += [(low, high), (high, low)]
    return lax.ppermute(block, axis, route)


def with_halo(block, sides, width, periodic):
    for axis, dim in sides:
        count = lax.axis_size(axis)
        forward = [(i, i + 1) for i in range(count - 1)]
        if periodic:
            forward.append((count - 1, 0))
        backward = [(target, source) for source, target in forward]
        low = lax.ppermute(
            lax.slice_in_dim(block, block.shape[dim] - width, None, axis=dim), axis, forward
        )
        high = lax.ppermute(lax.slice_in_dim(block, 0, width, axis=dim), axis, backward)
        block = jnp.concatenate([low, block, high], axis=dim)
    return block


def operators(
    center, radial_plus, radial_minus, theta_plus, theta_minus, axial_plus, axial_minus, total_theta
):
    radius = jnp.arange(center.shape[-1], dtype=jnp.float32) + 0.5
    step_angle = 2.0 * jnp.pi / total_theta
    d_radial = (radial_plus - radial_minus) * 0.5
    d_theta = (theta_plus - theta_minus) / (2.0 * step_angle)
    d_axial = (axial_plus - axial_minus) * 0.5
    laplace = (
        radial_plus - 2.0 * center + radial_minus + (radial_plus - radial_minus) / (2.0 * radius)
    )
    laplace = laplace + (theta_plus - 2.0 * center + theta_minus) / (
        radius * radius * step_angle * step_angle
    )
    laplace = laplace + axial_plus - 2.0 * center + axial_minus
    return (d_radial, d_theta, d_axial, laplace)


def on_device(fields):
    count_fields, planes, theta_dev, radial = fields.shape
    sectors = lax.axis_size("az")
    total_theta = theta_dev * sectors
    near = filtered(fields, sectors)
    state = jnp.concatenate([near, fields[:, :, :, LANES:]], axis=3)
    flip = jnp.array([-1.0, -1.0, 1.0, 1.0, 1.0], dtype=jnp.float32)[:, None, None]
    top_bit = sectors.bit_length() - 1
    opposite = swapped(state[:, :, :, 0], "az", top_bit - 1)
    opposite = opposite * flip
    theta_padded = with_halo(state, (("az", 2),), 1, True)
    axial_padded = with_halo(state, (("ax", 1),), 1, False)
    radial_plus = jnp.concatenate([state[:, :, :, 1:], jnp.zeros_like(state[:, :, :, :1])], axis=3)
    radial_minus = jnp.concatenate([opposite[:, :, :, None], state[:, :, :, :-1]], axis=3)
    d_radial, d_theta, d_axial, laplace = operators(
        state,
        radial_plus,
        radial_minus,
        theta_padded[:, :, 2:, :],
        theta_padded[:, :, :-2, :],
        axial_padded[:, 2:, :, :],
        axial_padded[:, :-2, :, :],
        total_theta,
    )
    radius = jnp.arange(radial, dtype=jnp.float32) + 0.5
    radial_u = state[0]
    theta_u = state[1]
    axial_u = state[2]
    change = (
        -(radial_u[None] * d_radial + (theta_u / radius)[None] * d_theta + axial_u[None] * d_axial)
        + viscosity * laplace
    )
    inverse_square = 1.0 / (radius * radius)
    first = (
        change[0]
        + theta_u * theta_u / radius
        - viscosity * (radial_u * inverse_square + 2.0 * inverse_square * d_theta[1])
    )
    second = (
        change[1]
        - radial_u * theta_u / radius
        - viscosity * (theta_u * inverse_square - 2.0 * inverse_square * d_theta[0])
    )
    third = change[2] + buoyancy * state[3]
    change = jnp.concatenate([first[None], second[None], third[None], change[3:]], axis=0)
    return state + time_step * change


def solution(mesh):
    placed = (P(None, "ax", "az", None),)
    return jax.shard_map(
        on_device, mesh=mesh, in_specs=placed, out_specs=P(None, "ax", "az", None), check_vma=False
    )
```

```python
import functools

import jax
import jax.numpy as jnp
import ml_dtypes
import numpy as np
from jax import lax
from jax.experimental import pallas as pl
from jax.experimental.pallas import tpu as pltpu
from jax.sharding import PartitionSpec as P

NEAR = 40
FIELDS = 5
MODES = 128
LANES = 128
HALF = 64
QUARTER = 10
TOP = 8
MESH = pl.DeviceIdType.MESH

viscosity = 0.2
time_step = 0.1
buoyancy = 1.0


def split(table, pieces):
    out = []
    rest = table.astype(np.float32)
    for _ in range(pieces):
        piece = rest.astype(ml_dtypes.bfloat16)
        out.append(piece)
        rest = rest - piece.astype(np.float32)
    return np.stack(out)


def basis(theta, total):
    mode = np.arange(MODES)
    angle = (theta[..., None] * mode % total) * (2.0 * np.pi / total)
    return np.concatenate([np.cos(angle), np.sin(angle)], axis=-1)


def transform_tables(sectors, theta_dev):
    total = sectors * theta_dev
    half = theta_dev // 2
    sector = np.arange(sectors)[:, None] * theta_dev
    mode = np.arange(MODES)
    weight = np.concatenate([np.where(mode == 0, 1.0, 2.0), np.full(MODES, 2.0)]) / total
    forward = []
    inverse = []
    for side in range(2):
        theta = (sector + side * half + np.arange(half)).reshape(-1)
        forward.append((basis(theta, total) * weight).T)
        first = sector + (half if side else -1)
        theta = np.concatenate([(first + np.arange(half)).reshape(-1), (first + half).reshape(-1)])
        inverse.append(basis(theta, total))
    return split(np.concatenate(forward, axis=0), 2), split(np.concatenate(inverse, axis=1), 3)


def stencil_kernel(
    sectors,
    slabs,
    fields,
    forward_hbm,
    inverse_hbm,
    advanced,
    state,
    across,
    result,
    forward,
    inverse,
    send1,
    recv1,
    send2,
    recv2,
    extra,
    edge_send,
    edge_recv,
    load_sem,
    store_sem,
    send_sem,
    recv_sem,
):
    me = lax.axis_index("az")
    slab = lax.axis_index("ax")
    planes = fields.shape[1]
    theta_dev = fields.shape[2]
    half = theta_dev // 2
    tiles = fields.shape[3] // LANES
    body = pl.ds(TOP, theta_dev)
    middle = TOP + half
    step_angle = 2.0 * np.pi / (sectors * theta_dev)

    loads = []
    for tile in range(tiles):
        loads.append(
            pltpu.make_async_copy(
                fields.at[:, :, :, pl.ds(tile * LANES, LANES)],
                state.at[tile, :, pl.ds(1, planes), body, :],
                load_sem.at[tile],
            )
        )
        loads[-1].start()
    load_forward = pltpu.make_async_copy(forward_hbm, forward, load_sem.at[tiles])
    load_forward.start()
    load_inverse = pltpu.make_async_copy(inverse_hbm, inverse, load_sem.at[tiles + 1])
    load_inverse.start()

    barrier = pltpu.get_barrier_semaphore()

    def greet(i, carry):
        pl.semaphore_signal(
            barrier, inc=1, device_id={"az": (me + i) % sectors}, device_id_type=MESH
        )
        return carry

    lax.fori_loop(1, sectors, greet, 0)
    above = (slab + 1) % slabs
    below = (slab + slabs - 1) % slabs
    for neighbour in (above, below):
        pl.semaphore_signal(barrier, inc=1, device_id={"ax": neighbour}, device_id_type=MESH)

    loads[0].wait()
    lane = lax.broadcasted_iota(jnp.int32, (half, LANES), 1)
    lane_row = lax.broadcasted_iota(jnp.int32, (1, LANES), 1)

    def pack(k, carry):
        tail0 = state[0, 4, k + 1, TOP:middle, :]
        tail1 = state[0, 4, k + 1, middle : middle + half, :]
        for f in range(4):
            shift = NEAR - QUARTER * f
            first = jnp.where(
                lane < NEAR, state[0, f, k + 1, TOP:middle, :], pltpu.roll(tail0, shift, 1)
            )
            second = jnp.where(
                lane < NEAR,
                state[0, f, k + 1, middle : middle + half, :],
                pltpu.roll(tail1, shift, 1),
            )
            send1[k * 4 + f] = jnp.where(lane < HALF, first, pltpu.roll(second, HALF, 1))
        return carry

    lax.fori_loop(0, planes, pack, 0)
    pl.semaphore_wait(barrier, sectors + 1)

    def exchange(source, target, index):
        def post(i, carry):
            peer = (me + i) % sectors
            pltpu.make_async_remote_copy(
                src_ref=source.at[peer],
                dst_ref=target.at[me],
                send_sem=send_sem.at[index],
                recv_sem=recv_sem.at[index],
                device_id={"az": peer},
                device_id_type=MESH,
            ).start()
            return carry

        lax.fori_loop(1, sectors, post, 0)
        target[me] = source[me]
        return pltpu.make_async_remote_copy(
            src_ref=source.at[pl.ds(0, sectors - 1)],
            dst_ref=target.at[pl.ds(0, sectors - 1)],
            send_sem=send_sem.at[index],
            recv_sem=recv_sem.at[index],
            device_id={"az": (me + 1) % sectors},
            device_id_type=MESH,
        )

    first_exchange = exchange(send1, recv1, 0)

    def plane_copy(first_tile, count, source, target, neighbour, index):
        return pltpu.make_async_remote_copy(
            src_ref=state.at[pl.ds(first_tile, count), :, source, body, :],
            dst_ref=state.at[pl.ds(first_tile, count), :, target, body, :],
            send_sem=send_sem.at[index],
            recv_sem=recv_sem.at[index],
            device_id={"ax": neighbour},
            device_id_type=MESH,
        )

    for load in loads[1:]:
        load.wait()
    far_planes = [
        plane_copy(1, tiles - 1, planes, 0, above, 2),
        plane_copy(1, tiles - 1, 1, planes + 1, below, 3),
    ]
    for copy in far_planes:
        copy.start()

    def collect(i, carry):
        tile = i // FIELDS
        f = i % FIELDS
        for k in range(planes):
            edge_send[0, tile, f, k : k + 1, :] = state[tile, f, k + 1, TOP : TOP + 1, :]
            edge_send[1, tile, f, k : k + 1, :] = state[
                tile, f, k + 1, TOP + theta_dev - 1 : TOP + theta_dev, :
            ]
        return carry

    lax.fori_loop(0, tiles * FIELDS, collect, 0)
    edges = []
    for side, peer in ((0, (me + sectors - 1) % sectors), (1, (me + 1) % sectors)):
        edges.append(
            pltpu.make_async_remote_copy(
                src_ref=edge_send.at[side],
                dst_ref=edge_recv.at[side],
                send_sem=send_sem.at[4 + side],
                recv_sem=recv_sem.at[4 + side],
                device_id={"az": peer},
                device_id_type=MESH,
            )
        )
        edges[-1].start()

    load_forward.wait()
    load_inverse.wait()
    first_exchange.wait_recv()
    values = recv1[...].reshape(sectors * half, LANES)
    high = values.astype(jnp.bfloat16)
    low = (values - high.astype(jnp.float32)).astype(jnp.bfloat16)
    dot = functools.partial(jnp.dot, preferred_element_type=jnp.float32)
    spectra = dot(forward[0], high) + (dot(forward[0], low) + dot(forward[1], high))
    row = lax.broadcasted_iota(jnp.int32, (2 * MODES, LANES), 0)
    column = lax.broadcasted_iota(jnp.int32, (2 * MODES, LANES), 1)
    spectra = jnp.where(column < HALF, spectra[: 2 * MODES], spectra[2 * MODES :])
    spectra = spectra + pltpu.roll(spectra, HALF, 1)
    slot = jnp.where(column < HALF, column, column - HALF)
    group = me % 4
    cycle = jnp.where(slot < NEAR, slot, slot - NEAR + QUARTER * group)
    cutoff = jnp.floor((355 * (2 * cycle + 1)).astype(jnp.float32) / 226.0 + 0.001)
    mode = jnp.where(row < MODES, row, row - MODES)
    kept = mode.astype(jnp.float32) <= jnp.minimum(cutoff, MODES - 1.0)
    spectra = jnp.where(kept, spectra, 0.0)
    parity = jnp.where(mode % 2 == 0, 1.0, -1.0)
    vector_sign = jnp.where(group < 2, -1.0, 1.0)
    spectra = jnp.where(
        slot == HALF - 1,
        parity * vector_sign * pltpu.roll(spectra, HALF - 1, 1),
        jnp.where(slot == HALF - 2, parity * pltpu.roll(spectra, HALF - 2 - NEAR, 1), spectra),
    )
    spectra = jnp.concatenate(
        [jnp.where(column < HALF, spectra, 0.0), jnp.where(column < HALF, 0.0, spectra)], axis=0
    )
    high = spectra.astype(jnp.bfloat16)
    rest = spectra - high.astype(jnp.float32)
    medium = rest.astype(jnp.bfloat16)
    low = (rest - medium.astype(jnp.float32)).astype(jnp.bfloat16)
    smooth = dot(inverse[0], low) + dot(inverse[1], medium) + dot(inverse[2], high)
    smooth = smooth + (dot(inverse[0], medium) + dot(inverse[1], high))
    smooth = smooth + dot(inverse[0], high)
    send2[:, 0:half, :] = smooth[: sectors * half].reshape(sectors, half, LANES)
    extra[...] = smooth[sectors * half :]

    def last_rows(i, carry):
        for d in range(8):
            send2[i * 8 + d, half : half + 1, :] = extra[pl.ds(i * 8 + d, 1), :]
        return carry

    lax.fori_loop(0, sectors // 8, last_rows, 0)
    second_exchange = exchange(send2, recv2, 1)

    for copy in edges + far_planes:
        copy.wait_recv()

    def spread(i, carry):
        tile = i // FIELDS
        f = i % FIELDS
        for k in range(planes):
            state[tile, f, k + 1, TOP - 1 : TOP, :] = edge_recv[1, tile, f, k : k + 1, :]
            state[tile, f, k + 1, TOP + theta_dev : TOP + theta_dev + 1, :] = edge_recv[
                0, tile, f, k : k + 1, :
            ]
        return carry

    lax.fori_loop(0, tiles * FIELDS, spread, 0)

    def close(first_tile, last_tile):
        nothing = jnp.zeros((theta_dev, LANES), jnp.float32)
        for plane, edge in ((0, 0), (planes + 1, slabs - 1)):

            @pl.when(slab == edge)
            def _():
                for tile in range(first_tile, last_tile):
                    for f in range(FIELDS):
                        state[tile, f, plane, body, :] = nothing

    close(1, tiles)
    lane_full = lax.broadcasted_iota(jnp.int32, (theta_dev, LANES), 1)

    def advance(tile, k):
        radius = (lane_row + tile * LANES).astype(jnp.float32) + 0.5
        inverse_radius = 1.0 / radius
        inverse_square = 1.0 / (radius * radius)
        spread_rate = time_step * viscosity
        radial_base = (0.5 * spread_rate) * inverse_radius
        theta_rate = (-time_step / (2.0 * step_angle)) * inverse_radius
        theta_spread = (spread_rate / (step_angle * step_angle)) * inverse_square
        turn_rate = time_step * inverse_radius
        swirl = spread_rate * inverse_square
        cross = (spread_rate / step_angle) * inverse_square
        center = [state[tile, f, k + 1, body, :] for f in range(FIELDS)]
        radial = radial_base - (0.5 * time_step) * center[0]
        around = theta_rate * center[1]
        axial = (-0.5 * time_step) * center[2]
        outs = []
        turns = []
        for f in range(FIELDS):
            q = center[f]
            inner = across[f, k] if tile == 0 else state[tile - 1, f, k + 1, body, :]
            outer = 0.0 if tile == tiles - 1 else state[tile + 1, f, k + 1, body, :]
            minus = pltpu.roll(jnp.where(lane_full == LANES - 1, inner, q), 1, 1)
            plus = pltpu.roll(jnp.where(lane_full == 0, outer, q), LANES - 1, 1)
            ahead = state[tile, f, k + 1, pl.ds(TOP + 1, theta_dev), :] - q
            behind = state[tile, f, k + 1, pl.ds(TOP - 1, theta_dev), :] - q
            up = state[tile, f, k + 2, body, :]
            down = state[tile, f, k, body, :]
            turn = ahead - behind
            turns.append(turn)
            out = q + (plus - minus) * radial + turn * around + (up - down) * axial
            out = out + spread_rate * ((plus + minus) + (up + down) - 4.0 * q)
            outs.append(out + theta_spread * (ahead + behind))
        whirl = turn_rate * center[1]
        outs[0] = outs[0] + whirl * center[1] - swirl * center[0] - cross * turns[1]
        outs[1] = outs[1] - whirl * center[0] - swirl * center[1] + cross * turns[0]
        outs[2] = outs[2] + (time_step * buoyancy) * center[3]
        for f in range(FIELDS):
            result[tile, f, k] = outs[f]

    stores = []

    def store(tile):
        stores.append(
            pltpu.make_async_copy(
                result.at[tile],
                advanced.at[:, :, :, pl.ds(tile * LANES, LANES)],
                store_sem.at[tile],
            )
        )
        stores[-1].start()

    for tile in range(1, tiles):

        def far(k, carry):
            advance(tile, k)
            return carry

        lax.fori_loop(0, planes, far, 0)
        store(tile)

    second_exchange.wait_recv()

    def unpack(k):
        tail = [
            state[0, 4, k + 1, TOP:middle, :],
            state[0, 4, k + 1, middle : middle + half, :],
            state[0, 4, k + 1, TOP - 1 : TOP, :],
            state[0, 4, k + 1, TOP + theta_dev : TOP + theta_dev + 1, :],
        ]
        for f in range(4):
            got0 = recv2[k * 4 + f, 1 : half + 1, :]
            got1 = recv2[k * 4 + f, 0:half, :]
            got2 = recv2[k * 4 + f, 0:1, :]
            got3 = recv2[k * 4 + f, half : half + 1, :]
            turned = pltpu.roll(got1, HALF, 1)
            across[f, k, 0:half, :] = pltpu.roll(got0, HALF, 1)
            across[f, k, half:, :] = got1
            near = lane < NEAR
            near_row = lane_row < NEAR
            here = state.at[0, f, k + 1]
            here[TOP:middle, :] = jnp.where(near, got0, here[TOP:middle, :])
            here[middle : middle + half, :] = jnp.where(
                near, turned, here[middle : middle + half, :]
            )
            here[TOP - 1 : TOP, :] = jnp.where(near_row, got2, here[TOP - 1 : TOP, :])
            here[TOP + theta_dev : TOP + theta_dev + 1, :] = jnp.where(
                near_row,
                pltpu.roll(got3, HALF, 1),
                here[TOP + theta_dev : TOP + theta_dev + 1, :],
            )
            shift = (QUARTER * f - NEAR) % LANES
            other = (shift + HALF) % LANES
            part = (lane >= QUARTER * f) & (lane < QUARTER * (f + 1))
            part_row = (lane_row >= QUARTER * f) & (lane_row < QUARTER * (f + 1))
            tail[0] = jnp.where(part, pltpu.roll(got0, shift, 1), tail[0])
            tail[1] = jnp.where(part, pltpu.roll(got1, other, 1), tail[1])
            tail[2] = jnp.where(part_row, pltpu.roll(got2, shift, 1), tail[2])
            tail[3] = jnp.where(part_row, pltpu.roll(got3, other, 1), tail[3])
            if f == 0:
                across[4, k, 0:half, :] = pltpu.roll(got0, HALF + 1, 1)
                across[4, k, half:, :] = pltpu.roll(got1, 1, 1)
        state[0, 4, k + 1, TOP:middle, :] = tail[0]
        state[0, 4, k + 1, middle : middle + half, :] = tail[1]
        state[0, 4, k + 1, TOP - 1 : TOP, :] = tail[2]
        state[0, 4, k + 1, TOP + theta_dev : TOP + theta_dev + 1, :] = tail[3]

    unpack(0)
    unpack(planes - 1)
    near_planes = [
        plane_copy(0, 1, planes, 0, above, 6),
        plane_copy(0, 1, 1, planes + 1, below, 7),
    ]
    for copy in near_planes:
        copy.start()

    def unpack_inner(k, carry):
        unpack(k)
        return carry

    lax.fori_loop(1, planes - 1, unpack_inner, 0)

    def near(k, carry):
        advance(0, k)
        return carry

    lax.fori_loop(1, planes - 1, near, 0)
    for copy in near_planes:
        copy.wait_recv()
    close(0, 1)
    advance(0, 0)
    advance(0, planes - 1)
    store(0)
    first_exchange.wait_send()
    second_exchange.wait_send()
    for copy in edges + far_planes + near_planes:
        copy.wait_send()
    for copy in stores:
        copy.wait()


def on_device(fields):
    sectors = lax.axis_size("az")
    slabs = lax.axis_size("ax")
    count, planes, theta_dev, radial = fields.shape
    half = theta_dev // 2
    tiles = radial // LANES
    forward, inverse = transform_tables(sectors, theta_dev)
    hbm = pl.BlockSpec(memory_space=pltpu.HBM)
    return pl.pallas_call(
        functools.partial(stencil_kernel, sectors, slabs),
        out_shape=jax.ShapeDtypeStruct(fields.shape, jnp.float32),
        in_specs=[hbm, hbm, hbm],
        out_specs=hbm,
        scratch_shapes=[
            pltpu.VMEM((tiles, count, planes + 2, theta_dev + 2 * TOP, LANES), jnp.float32),
            pltpu.VMEM((count, planes, theta_dev, LANES), jnp.float32),
            pltpu.VMEM((tiles, count, planes, theta_dev, LANES), jnp.float32),
            pltpu.VMEM(forward.shape, jnp.bfloat16),
            pltpu.VMEM(inverse.shape, jnp.bfloat16),
            pltpu.VMEM((sectors, half, LANES), jnp.float32),
            pltpu.VMEM((sectors, half, LANES), jnp.float32),
            pltpu.VMEM((sectors, half + 1, LANES), jnp.float32),
            pltpu.VMEM((sectors, half + 1, LANES), jnp.float32),
            pltpu.VMEM((sectors, LANES), jnp.float32),
            pltpu.VMEM((2, tiles, count, planes, LANES), jnp.float32),
            pltpu.VMEM((2, tiles, count, planes, LANES), jnp.float32),
            pltpu.SemaphoreType.DMA((tiles + 2,)),
            pltpu.SemaphoreType.DMA((tiles,)),
            pltpu.SemaphoreType.DMA((8,)),
            pltpu.SemaphoreType.DMA((8,)),
        ],
        compiler_params=pltpu.CompilerParams(
            collective_id=0, has_side_effects=True, vmem_limit_bytes=48 << 20
        ),
        name="plume_section",
    )(fields, jnp.asarray(forward), jnp.asarray(inverse))


def solution(mesh):
    placed = (P(None, "ax", "az", None),)
    return jax.shard_map(
        on_device, mesh=mesh, in_specs=placed, out_specs=P(None, "ax", "az", None), check_vma=False
    )
```

```python
import functools

import jax
import jax.numpy as jnp
import ml_dtypes
import numpy as np
from jax import lax
from jax.experimental import pallas as pl
from jax.experimental.pallas import tpu as pltpu
from jax.sharding import PartitionSpec as P

NEAR = 40
FIELDS = 5
MODES = 128
LANES = 128
HALF = 64
QUARTER = 10
TOP = 8
MESH = pl.DeviceIdType.MESH

viscosity = 0.2
time_step = 0.1
buoyancy = 1.0


def split(table, pieces):
    out = []
    rest = table.astype(np.float32)
    for _ in range(pieces):
        piece = rest.astype(ml_dtypes.bfloat16)
        out.append(piece)
        rest = rest - piece.astype(np.float32)
    return np.stack(out)


def basis(theta, parity, total):
    mode = np.arange(parity, MODES, 2)
    angle = (theta[..., None] * mode % total) * (2.0 * np.pi / total)
    return np.concatenate([np.cos(angle), np.sin(angle)], axis=-1)


def transform_tables(sectors, theta_dev):
    total = sectors * theta_dev
    half = theta_dev // 2
    sector = np.arange(sectors // 2)[:, None] * theta_dev
    forward = []
    inverse = []
    for parity in range(2):
        mode = np.arange(parity, MODES, 2)
        weight = np.concatenate([np.where(mode == 0, 1.0, 2.0), np.full(MODES // 2, 2.0)]) / total
        into = []
        back = []
        for side in range(2):
            theta = (sector + side * half + np.arange(half)).reshape(-1)
            into.append((basis(theta, parity, total) * weight).T)
            first = sector + (half if side else -1)
            theta = np.concatenate(
                [(first + np.arange(half)).reshape(-1), (first + half).reshape(-1)]
            )
            back.append(basis(theta, parity, total))
        forward.append(split(np.concatenate(into, axis=0), 2))
        inverse.append(split(np.concatenate(back, axis=1), 3))
    return np.stack(forward), np.stack(inverse)


def stencil_kernel(
    sectors,
    slabs,
    fields,
    forward_hbm,
    inverse_hbm,
    advanced,
    state,
    across,
    result,
    forward,
    inverse,
    send1,
    recv1,
    send2,
    recv2,
    extra,
    edge_send,
    edge_recv,
    load_sem,
    store_sem,
    send_sem,
    recv_sem,
):
    me = lax.axis_index("az")
    slab = lax.axis_index("ax")
    planes = fields.shape[1]
    theta_dev = fields.shape[2]
    half = theta_dev // 2
    tiles = fields.shape[3] // LANES
    body = pl.ds(TOP, theta_dev)
    middle = TOP + half
    step_angle = 2.0 * np.pi / (sectors * theta_dev)

    loads = []
    for tile in range(tiles):
        loads.append(
            pltpu.make_async_copy(
                fields.at[:, :, :, pl.ds(tile * LANES, LANES)],
                state.at[tile, :, pl.ds(1, planes), body, :],
                load_sem.at[tile],
            )
        )
        loads[-1].start()
    load_forward = pltpu.make_async_copy(forward_hbm, forward, load_sem.at[tiles])
    load_forward.start()
    load_inverse = pltpu.make_async_copy(inverse_hbm, inverse, load_sem.at[tiles + 1])
    load_inverse.start()

    partner = (slab + slabs // 2) % slabs
    above = (slab + 1) % slabs
    below = (slab + slabs - 1) % slabs
    ahead = (me + 1) % sectors
    behind = (me + sectors - 1) % sectors
    own_x = me // 16
    own_y = me // 8 % 2
    own_z = me % 8

    def visit(call):
        def one(i, carry):
            step_x = (2 + (1 - 2 * (i // 16 % 2)) * ((i // 16 + 1) // 2)) % 4
            rest = i % 16 // 2
            step_z = 4 + (1 - 2 * (rest % 2)) * ((rest + 1) // 2)
            peer = (own_x + step_x) % 4 * 16 + (own_y + i) % 2 * 8 + (own_z + step_z) % 8
            call(peer)
            return carry

        lax.fori_loop(0, sectors, one, 0)

    barrier = pltpu.get_barrier_semaphore()

    def greet(peer):
        pl.semaphore_signal(
            barrier, inc=1, device_id={"az": peer, "ax": partner}, device_id_type=MESH
        )

    visit(greet)
    for neighbour in (above, below):
        pl.semaphore_signal(barrier, inc=1, device_id={"ax": neighbour}, device_id_type=MESH)
    for neighbour in (ahead, behind):
        pl.semaphore_signal(barrier, inc=1, device_id={"az": neighbour}, device_id_type=MESH)

    loads[0].wait()
    lane = lax.broadcasted_iota(jnp.int32, (half, LANES), 1)
    lane_row = lax.broadcasted_iota(jnp.int32, (1, LANES), 1)

    def pack(k, carry):
        tail0 = state[0, 4, k + 1, TOP:middle, :]
        tail1 = state[0, 4, k + 1, middle : middle + half, :]
        for f in range(4):
            shift = NEAR - QUARTER * f
            first = jnp.where(
                lane < NEAR, state[0, f, k + 1, TOP:middle, :], pltpu.roll(tail0, shift, 1)
            )
            second = jnp.where(
                lane < NEAR,
                state[0, f, k + 1, middle : middle + half, :],
                pltpu.roll(tail1, shift, 1),
            )
            send1[k * 4 + f] = jnp.where(lane < HALF, first, pltpu.roll(second, HALF, 1))
        return carry

    lax.fori_loop(0, planes, pack, 0)
    pl.semaphore_wait(barrier, sectors + 4)

    def exchange(source, target, index):
        def post(peer):
            pltpu.make_async_remote_copy(
                src_ref=source.at[peer],
                dst_ref=target.at[me],
                send_sem=send_sem.at[index],
                recv_sem=recv_sem.at[index],
                device_id={"az": peer, "ax": partner},
                device_id_type=MESH,
            ).start()

        visit(post)
        return pltpu.make_async_remote_copy(
            src_ref=source,
            dst_ref=target,
            send_sem=send_sem.at[index],
            recv_sem=recv_sem.at[index],
            device_id={"az": me, "ax": partner},
            device_id_type=MESH,
        )

    first_exchange = exchange(send1, recv1, 0)

    def plane_copy(first_tile, count, source, target, neighbour, index):
        return pltpu.make_async_remote_copy(
            src_ref=state.at[pl.ds(first_tile, count), :, source, body, :],
            dst_ref=state.at[pl.ds(first_tile, count), :, target, body, :],
            send_sem=send_sem.at[index],
            recv_sem=recv_sem.at[index],
            device_id={"ax": neighbour},
            device_id_type=MESH,
        )

    for load in loads[1:]:
        load.wait()
    far_planes = [
        plane_copy(1, tiles - 1, planes, 0, above, 2),
        plane_copy(1, tiles - 1, 1, planes + 1, below, 3),
    ]
    for copy in far_planes:
        copy.start()

    def collect(i, carry):
        tile = i // FIELDS
        f = i % FIELDS
        for k in range(planes):
            edge_send[0, tile, f, k : k + 1, :] = state[tile, f, k + 1, TOP : TOP + 1, :]
            edge_send[1, tile, f, k : k + 1, :] = state[
                tile, f, k + 1, TOP + theta_dev - 1 : TOP + theta_dev, :
            ]
        return carry

    lax.fori_loop(0, tiles * FIELDS, collect, 0)
    edges = []
    for side, peer in ((0, behind), (1, ahead)):
        edges.append(
            pltpu.make_async_remote_copy(
                src_ref=edge_send.at[side],
                dst_ref=edge_recv.at[side],
                send_sem=send_sem.at[4 + side],
                recv_sem=recv_sem.at[4 + side],
                device_id={"az": peer},
                device_id_type=MESH,
            )
        )
        edges[-1].start()

    load_forward.wait()
    load_inverse.wait()
    first_exchange.wait_recv()
    dot = functools.partial(jnp.dot, preferred_element_type=jnp.float32)
    pairs = sectors // 2
    row = lax.broadcasted_iota(jnp.int32, (MODES, LANES), 0)
    column = lax.broadcasted_iota(jnp.int32, (MODES, LANES), 1)
    slot = jnp.where(column < HALF, column, column - HALF)
    group = me % 4
    cycle = jnp.where(slot < NEAR, slot, slot - NEAR + QUARTER * group)
    cutoff = jnp.floor((355 * (2 * cycle + 1)).astype(jnp.float32) / 226.0 + 0.001)
    cutoff = jnp.minimum(cutoff, MODES - 1.0)
    vector_sign = jnp.where(group < 2, -1.0, 1.0)
    smooth = []
    for parity in range(2):
        near_half = recv1[0:pairs].reshape(pairs * half, LANES)
        far_half = recv1[pairs:].reshape(pairs * half, LANES)
        values = near_half - far_half if parity else near_half + far_half
        high = values.astype(jnp.bfloat16)
        low = (values - high.astype(jnp.float32)).astype(jnp.bfloat16)
        both = dot(forward[parity, 0], jnp.concatenate([high, low], axis=1))
        spectra = both[:, :LANES] + (both[:, LANES:] + dot(forward[parity, 1], high))
        spectra = jnp.where(column < HALF, spectra[:MODES], spectra[MODES:])
        spectra = spectra + pltpu.roll(spectra, HALF, 1)
        mode = 2 * jnp.where(row < MODES // 2, row, row - MODES // 2) + parity
        spectra = jnp.where(mode.astype(jnp.float32) <= cutoff, spectra, 0.0)
        sign = -1.0 if parity else 1.0
        spectra = jnp.where(
            slot == HALF - 1,
            (sign * vector_sign) * pltpu.roll(spectra, HALF - 1, 1),
            jnp.where(slot == HALF - 2, sign * pltpu.roll(spectra, HALF - 2 - NEAR, 1), spectra),
        )
        spectra = jnp.concatenate(
            [jnp.where(column < HALF, spectra, 0.0), jnp.where(column < HALF, 0.0, spectra)],
            axis=0,
        )
        high = spectra.astype(jnp.bfloat16)
        rest = spectra - high.astype(jnp.float32)
        medium = rest.astype(jnp.bfloat16)
        low = (rest - medium.astype(jnp.float32)).astype(jnp.bfloat16)
        wide = jnp.concatenate([high, medium], axis=1)
        first = dot(inverse[parity, 0], wide)
        second = dot(inverse[parity, 1], wide)
        third = dot(inverse[parity, 0], low) + dot(inverse[parity, 2], high)
        third = third + second[:, LANES:]
        smooth.append(first[:, :LANES] + (first[:, LANES:] + second[:, :LANES] + third))
    for side in range(2):
        value = smooth[0] - smooth[1] if side else smooth[0] + smooth[1]
        send2[side * pairs : (side + 1) * pairs, 0:half, :] = value[: pairs * half].reshape(
            pairs, half, LANES
        )
        extra[side * pairs : (side + 1) * pairs, :] = value[pairs * half :]

    def last_rows(i, carry):
        for d in range(8):
            send2[i * 8 + d, half : half + 1, :] = extra[pl.ds(i * 8 + d, 1), :]
        return carry

    lax.fori_loop(0, sectors // 8, last_rows, 0)
    second_exchange = exchange(send2, recv2, 1)

    for copy in edges + far_planes:
        copy.wait_recv()

    def spread(i, carry):
        tile = i // FIELDS
        f = i % FIELDS
        for k in range(planes):
            state[tile, f, k + 1, TOP - 1 : TOP, :] = edge_recv[1, tile, f, k : k + 1, :]
            state[tile, f, k + 1, TOP + theta_dev : TOP + theta_dev + 1, :] = edge_recv[
                0, tile, f, k : k + 1, :
            ]
        return carry

    lax.fori_loop(0, tiles * FIELDS, spread, 0)

    def close(first_tile, last_tile):
        nothing = jnp.zeros((theta_dev, LANES), jnp.float32)
        for plane, edge in ((0, 0), (planes + 1, slabs - 1)):

            @pl.when(slab == edge)
            def _():
                for tile in range(first_tile, last_tile):
                    for f in range(FIELDS):
                        state[tile, f, plane, body, :] = nothing

    close(1, tiles)
    lane_full = lax.broadcasted_iota(jnp.int32, (theta_dev, LANES), 1)

    def advance(tile, k):
        radius = (lane_row + tile * LANES).astype(jnp.float32) + 0.5
        inverse_radius = 1.0 / radius
        inverse_square = 1.0 / (radius * radius)
        spread_rate = time_step * viscosity
        radial_base = (0.5 * spread_rate) * inverse_radius
        theta_rate = (-time_step / (2.0 * step_angle)) * inverse_radius
        theta_spread = (spread_rate / (step_angle * step_angle)) * inverse_square
        turn_rate = time_step * inverse_radius
        swirl = spread_rate * inverse_square
        cross = (spread_rate / step_angle) * inverse_square
        center = [state[tile, f, k + 1, body, :] for f in range(FIELDS)]
        radial = radial_base - (0.5 * time_step) * center[0]
        around = theta_rate * center[1]
        axial = (-0.5 * time_step) * center[2]
        outs = []
        turns = []
        for f in range(FIELDS):
            q = center[f]
            inner = across[f, k] if tile == 0 else state[tile - 1, f, k + 1, body, :]
            outer = 0.0 if tile == tiles - 1 else state[tile + 1, f, k + 1, body, :]
            minus = pltpu.roll(jnp.where(lane_full == LANES - 1, inner, q), 1, 1)
            plus = pltpu.roll(jnp.where(lane_full == 0, outer, q), LANES - 1, 1)
            ahead = state[tile, f, k + 1, pl.ds(TOP + 1, theta_dev), :] - q
            behind = state[tile, f, k + 1, pl.ds(TOP - 1, theta_dev), :] - q
            up = state[tile, f, k + 2, body, :]
            down = state[tile, f, k, body, :]
            turn = ahead - behind
            turns.append(turn)
            out = q + (plus - minus) * radial + turn * around + (up - down) * axial
            out = out + spread_rate * ((plus + minus) + (up + down) - 4.0 * q)
            outs.append(out + theta_spread * (ahead + behind))
        whirl = turn_rate * center[1]
        outs[0] = outs[0] + whirl * center[1] - swirl * center[0] - cross * turns[1]
        outs[1] = outs[1] - whirl * center[0] - swirl * center[1] + cross * turns[0]
        outs[2] = outs[2] + (time_step * buoyancy) * center[3]
        for f in range(FIELDS):
            result[tile, f, k] = outs[f]

    stores = []

    def store(tile, first_plane, count):
        stores.append(
            pltpu.make_async_copy(
                result.at[tile, :, pl.ds(first_plane, count)],
                advanced.at[:, pl.ds(first_plane, count), :, pl.ds(tile * LANES, LANES)],
                store_sem.at[len(stores)],
            )
        )
        stores[-1].start()

    for tile in range(1, tiles):

        def far(k, carry):
            advance(tile, k)
            return carry

        lax.fori_loop(0, planes, far, 0)
        store(tile, 0, planes)

    second_exchange.wait_recv()

    def unpack(k):
        tail = [
            state[0, 4, k + 1, TOP:middle, :],
            state[0, 4, k + 1, middle : middle + half, :],
            state[0, 4, k + 1, TOP - 1 : TOP, :],
            state[0, 4, k + 1, TOP + theta_dev : TOP + theta_dev + 1, :],
        ]
        for f in range(4):
            got0 = recv2[k * 4 + f, 1 : half + 1, :]
            got1 = recv2[k * 4 + f, 0:half, :]
            got2 = recv2[k * 4 + f, 0:1, :]
            got3 = recv2[k * 4 + f, half : half + 1, :]
            turned = pltpu.roll(got1, HALF, 1)
            across[f, k, 0:half, :] = pltpu.roll(got0, HALF, 1)
            across[f, k, half:, :] = got1
            near = lane < NEAR
            near_row = lane_row < NEAR
            here = state.at[0, f, k + 1]
            here[TOP:middle, :] = jnp.where(near, got0, here[TOP:middle, :])
            here[middle : middle + half, :] = jnp.where(
                near, turned, here[middle : middle + half, :]
            )
            here[TOP - 1 : TOP, :] = jnp.where(near_row, got2, here[TOP - 1 : TOP, :])
            here[TOP + theta_dev : TOP + theta_dev + 1, :] = jnp.where(
                near_row,
                pltpu.roll(got3, HALF, 1),
                here[TOP + theta_dev : TOP + theta_dev + 1, :],
            )
            shift = (QUARTER * f - NEAR) % LANES
            other = (shift + HALF) % LANES
            part = (lane >= QUARTER * f) & (lane < QUARTER * (f + 1))
            part_row = (lane_row >= QUARTER * f) & (lane_row < QUARTER * (f + 1))
            tail[0] = jnp.where(part, pltpu.roll(got0, shift, 1), tail[0])
            tail[1] = jnp.where(part, pltpu.roll(got1, other, 1), tail[1])
            tail[2] = jnp.where(part_row, pltpu.roll(got2, shift, 1), tail[2])
            tail[3] = jnp.where(part_row, pltpu.roll(got3, other, 1), tail[3])
            if f == 0:
                across[4, k, 0:half, :] = pltpu.roll(got0, HALF + 1, 1)
                across[4, k, half:, :] = pltpu.roll(got1, 1, 1)
        state[0, 4, k + 1, TOP:middle, :] = tail[0]
        state[0, 4, k + 1, middle : middle + half, :] = tail[1]
        state[0, 4, k + 1, TOP - 1 : TOP, :] = tail[2]
        state[0, 4, k + 1, TOP + theta_dev : TOP + theta_dev + 1, :] = tail[3]

    unpack(0)
    unpack(planes - 1)
    near_planes = [
        plane_copy(0, 1, planes, 0, above, 6),
        plane_copy(0, 1, 1, planes + 1, below, 7),
    ]
    for copy in near_planes:
        copy.start()

    def unpack_inner(k, carry):
        unpack(k)
        return carry

    lax.fori_loop(1, planes - 1, unpack_inner, 0)

    def near(k, carry):
        advance(0, k)
        return carry

    lax.fori_loop(1, planes - 1, near, 0)
    store(0, 1, planes - 2)
    for copy in near_planes:
        copy.wait_recv()
    close(0, 1)
    advance(0, 0)
    store(0, 0, 1)
    advance(0, planes - 1)
    store(0, planes - 1, 1)
    first_exchange.wait_send()
    second_exchange.wait_send()
    for copy in edges + far_planes + near_planes:
        copy.wait_send()
    for copy in stores:
        copy.wait()


def on_device(fields):
    sectors = lax.axis_size("az")
    slabs = lax.axis_size("ax")
    count, planes, theta_dev, radial = fields.shape
    half = theta_dev // 2
    tiles = radial // LANES
    forward, inverse = transform_tables(sectors, theta_dev)
    hbm = pl.BlockSpec(memory_space=pltpu.HBM)
    return pl.pallas_call(
        functools.partial(stencil_kernel, sectors, slabs),
        out_shape=jax.ShapeDtypeStruct(fields.shape, jnp.float32),
        in_specs=[hbm, hbm, hbm],
        out_specs=hbm,
        scratch_shapes=[
            pltpu.VMEM((tiles, count, planes + 2, theta_dev + 2 * TOP, LANES), jnp.float32),
            pltpu.VMEM((count, planes, theta_dev, LANES), jnp.float32),
            pltpu.VMEM((tiles, count, planes, theta_dev, LANES), jnp.float32),
            pltpu.VMEM(forward.shape, jnp.bfloat16),
            pltpu.VMEM(inverse.shape, jnp.bfloat16),
            pltpu.VMEM((sectors, half, LANES), jnp.float32),
            pltpu.VMEM((sectors, half, LANES), jnp.float32),
            pltpu.VMEM((sectors, half + 1, LANES), jnp.float32),
            pltpu.VMEM((sectors, half + 1, LANES), jnp.float32),
            pltpu.VMEM((sectors, LANES), jnp.float32),
            pltpu.VMEM((2, tiles, count, planes, LANES), jnp.float32),
            pltpu.VMEM((2, tiles, count, planes, LANES), jnp.float32),
            pltpu.SemaphoreType.DMA((tiles + 2,)),
            pltpu.SemaphoreType.DMA((tiles + 2,)),
            pltpu.SemaphoreType.DMA((8,)),
            pltpu.SemaphoreType.DMA((8,)),
        ],
        compiler_params=pltpu.CompilerParams(
            collective_id=0, has_side_effects=True, vmem_limit_bytes=48 << 20
        ),
        name="plume_section",
    )(
        pltpu.with_memory_space_constraint(fields, pltpu.HBM),
        pltpu.with_memory_space_constraint(jnp.asarray(forward), pltpu.HBM),
        pltpu.with_memory_space_constraint(jnp.asarray(inverse), pltpu.HBM),
    )


def solution(mesh):
    placed = (P(None, "ax", "az", None),)
    return jax.shard_map(
        on_device, mesh=mesh, in_specs=placed, out_specs=P(None, "ax", "az", None), check_vma=False
    )
```

```python
import functools

import jax
import jax.numpy as jnp
import ml_dtypes
import numpy as np
from jax import lax
from jax.experimental import pallas as pl
from jax.experimental.pallas import tpu as pltpu
from jax.sharding import PartitionSpec as P

NEAR = 40
FIELDS = 5
MODES = 128
LANES = 128
HALF = 64
QUARTER = 10
SPAN = 7
ORDER = (0, 1, 3, 2)
TOP = 8
MESH = pl.DeviceIdType.MESH

viscosity = 0.2
time_step = 0.1
buoyancy = 1.0


def split(table, pieces):
    out = []
    rest = table.astype(np.float32)
    for _ in range(pieces):
        piece = rest.astype(ml_dtypes.bfloat16)
        out.append(piece)
        rest = rest - piece.astype(np.float32)
    return np.stack(out)


def basis(theta, parity, total):
    mode = np.arange(parity, MODES, 2)
    angle = (theta[..., None] * mode % total) * (2.0 * np.pi / total)
    return np.concatenate([np.cos(angle), np.sin(angle)], axis=-1)


def transform_tables(sectors, theta_dev):
    total = sectors * theta_dev
    half = theta_dev // 2
    sector = np.arange(sectors // 2)[:, None] * theta_dev
    forward = []
    inverse = []
    for parity in range(2):
        mode = np.arange(parity, MODES, 2)
        weight = np.concatenate([np.where(mode == 0, 1.0, 2.0), np.full(MODES // 2, 2.0)]) / total
        into = []
        back = []
        for side in range(2):
            theta = (sector + side * half + np.arange(half)).reshape(-1)
            into.append((basis(theta, parity, total) * weight).T)
            edge = sector + (theta_dev if side else -1)
            theta = np.concatenate([theta, edge.reshape(-1)])
            back.append(basis(theta, parity, total))
        forward.append(split(np.concatenate(into, axis=0), 2))
        inverse.append(split(np.concatenate(back, axis=1), 3))
    return np.stack(forward), np.stack(inverse)


def stencil_kernel(
    sectors,
    slabs,
    fields,
    forward_hbm,
    inverse_hbm,
    advanced,
    state,
    across,
    result,
    forward,
    inverse,
    send1,
    recv1,
    send2,
    recv2,
    extra,
    ghost,
    edge_send,
    edge_recv,
    load_sem,
    store_sem,
    send_sem,
    recv_sem,
):
    me = lax.axis_index("az")
    slab = lax.axis_index("ax")
    planes = fields.shape[1]
    theta_dev = fields.shape[2]
    half = theta_dev // 2
    tiles = fields.shape[3] // LANES
    body = pl.ds(TOP, theta_dev)
    middle = TOP + half
    step_angle = 2.0 * np.pi / (sectors * theta_dev)

    partner = (slab + slabs // 2) % slabs
    above = (slab + 1) % slabs
    below = (slab + slabs - 1) % slabs
    ahead = (me + 1) % sectors
    behind = (me + sectors - 1) % sectors
    own_x = me // 16
    own_y = me // 8 % 2
    own_z = me % 8

    own_group = own_z // 2
    own_plane = me // 8 * 2 + me % 2
    served = partner
    serves_below = (own_plane == 0) & (served > 0)
    serves_above = (own_plane == planes - 1) & (served < slabs - 1)
    serves_edge = serves_below | serves_above

    def owner(k, f):
        return k // 2 * 8 + 2 * f + k % 2

    def visit(call):
        def one(i, carry):
            step_x = (2 + (1 - 2 * (i // 16 % 2)) * ((i // 16 + 1) // 2)) % 4
            rest = i % 16 // 2
            step_z = 4 + (1 - 2 * (rest % 2)) * ((rest + 1) // 2)
            peer = (own_x + step_x) % 4 * 16 + (own_y + i) % 2 * 8 + (own_z + step_z) % 8
            call(peer)
            return carry

        lax.fori_loop(0, sectors, one, 0)

    barrier = pltpu.get_barrier_semaphore()

    def greet(peer):
        pl.semaphore_signal(
            barrier, inc=1, device_id={"az": peer, "ax": partner}, device_id_type=MESH
        )

    visit(greet)
    for neighbour in (above, below):
        pl.semaphore_signal(barrier, inc=1, device_id={"ax": neighbour}, device_id_type=MESH)
    for neighbour in (ahead, behind):
        pl.semaphore_signal(barrier, inc=1, device_id={"az": neighbour}, device_id_type=MESH)

    for f in range(4):

        @pl.when(slab < slabs - 1)
        def _():
            pl.semaphore_signal(
                barrier,
                inc=1,
                device_id={"az": owner(0, f), "ax": (slab + 1 + slabs // 2) % slabs},
                device_id_type=MESH,
            )

        @pl.when(slab > 0)
        def _():
            pl.semaphore_signal(
                barrier,
                inc=1,
                device_id={"az": owner(planes - 1, f), "ax": (slab + slabs // 2 - 1) % slabs},
                device_id_type=MESH,
            )

    loads = []
    for tile in range(tiles):
        loads.append(
            pltpu.make_async_copy(
                fields.at[:, :, :, pl.ds(tile * LANES, LANES)],
                state.at[tile, :, pl.ds(1, planes), body, :],
                load_sem.at[tile],
            )
        )
        loads[-1].start()
    load_forward = pltpu.make_async_copy(forward_hbm, forward, load_sem.at[tiles])
    load_forward.start()
    load_inverse = pltpu.make_async_copy(inverse_hbm, inverse, load_sem.at[tiles + 1])
    load_inverse.start()

    loads[0].wait()
    lane = lax.broadcasted_iota(jnp.int32, (half, LANES), 1)
    lane_row = lax.broadcasted_iota(jnp.int32, (1, LANES), 1)

    def pack(k, carry):
        tail0 = state[0, 4, k + 1, TOP:middle, :]
        tail1 = state[0, 4, k + 1, middle : middle + half, :]
        for f in range(4):
            shift = NEAR - QUARTER * f
            first = jnp.where(
                lane < NEAR, state[0, f, k + 1, TOP:middle, :], pltpu.roll(tail0, shift, 1)
            )
            second = jnp.where(
                lane < NEAR,
                state[0, f, k + 1, middle : middle + half, :],
                pltpu.roll(tail1, shift, 1),
            )
            send1[owner(k, f)] = jnp.where(lane < HALF, first, pltpu.roll(second, HALF, 1))
        return carry

    lax.fori_loop(0, planes, pack, 0)
    pl.semaphore_wait(barrier, sectors + 4 + jnp.where(serves_edge, sectors, 0))

    def exchange(source, target, index, arrival):
        def post(peer):
            pltpu.make_async_remote_copy(
                src_ref=source.at[peer],
                dst_ref=target.at[me],
                send_sem=send_sem.at[index],
                recv_sem=recv_sem.at[arrival],
                device_id={"az": peer, "ax": partner},
                device_id_type=MESH,
            ).start()

        visit(post)

    def whole(buffer, count, index, arrival):
        return pltpu.make_async_remote_copy(
            src_ref=buffer.at[pl.ds(0, count)],
            dst_ref=buffer.at[pl.ds(0, count)],
            send_sem=send_sem.at[index],
            recv_sem=recv_sem.at[arrival],
            device_id={"az": me, "ax": partner},
            device_id_type=MESH,
        )

    exchange(send1, recv1, 0, 0)

    def plane_copy(first_tile, count, source, target, neighbour, index):
        return pltpu.make_async_remote_copy(
            src_ref=state.at[pl.ds(first_tile, count), :, source, body, :],
            dst_ref=state.at[pl.ds(first_tile, count), :, target, body, :],
            send_sem=send_sem.at[index],
            recv_sem=recv_sem.at[index],
            device_id={"ax": neighbour},
            device_id_type=MESH,
        )

    for load in loads[1:]:
        load.wait()
    far_planes = [
        plane_copy(0, tiles, planes, 0, above, 2),
        plane_copy(0, tiles, 1, planes + 1, below, 3),
    ]
    for copy in far_planes:
        copy.start()

    def collect(i, carry):
        tile = i // FIELDS
        f = i % FIELDS
        for k in range(planes):
            edge_send[0, tile, f, k : k + 1, :] = state[tile, f, k + 1, TOP : TOP + 1, :]
            edge_send[1, tile, f, k : k + 1, :] = state[
                tile, f, k + 1, TOP + theta_dev - 1 : TOP + theta_dev, :
            ]
        return carry

    lax.fori_loop(0, tiles * FIELDS, collect, 0)
    edges = []
    for side, peer in ((0, behind), (1, ahead)):
        edges.append(
            pltpu.make_async_remote_copy(
                src_ref=edge_send.at[side],
                dst_ref=edge_recv.at[side],
                send_sem=send_sem.at[4 + side],
                recv_sem=recv_sem.at[4 + side],
                device_id={"az": peer},
                device_id_type=MESH,
            )
        )
        edges[-1].start()

    load_forward.wait()
    load_inverse.wait()
    whole(recv1, sectors, 0, 0).wait_recv()
    dot = functools.partial(jnp.dot, preferred_element_type=jnp.float32)
    pairs = sectors // 2
    row = lax.broadcasted_iota(jnp.int32, (MODES, LANES), 0)
    column = lax.broadcasted_iota(jnp.int32, (MODES, LANES), 1)
    slot = jnp.where(column < HALF, column, column - HALF)
    group = own_group
    cycle = jnp.where(slot < NEAR, slot, slot - NEAR + QUARTER * group)
    cutoff = jnp.floor((355 * (2 * cycle + 1)).astype(jnp.float32) / 226.0 + 0.001)
    cutoff = jnp.minimum(cutoff, MODES - 1.0)
    vector_sign = jnp.where(group < 2, -1.0, 1.0)
    smooth = []
    for parity in range(2):
        near_half = recv1[0:pairs].reshape(pairs * half, LANES)
        far_half = recv1[pairs:].reshape(pairs * half, LANES)
        values = near_half - far_half if parity else near_half + far_half
        high = values.astype(jnp.bfloat16)
        low = (values - high.astype(jnp.float32)).astype(jnp.bfloat16)
        both = dot(forward[parity, 0], jnp.concatenate([high, low], axis=1))
        spectra = both[:, :LANES] + (both[:, LANES:] + dot(forward[parity, 1], high))
        spectra = jnp.where(column < HALF, spectra[:MODES], spectra[MODES:])
        spectra = spectra + pltpu.roll(spectra, HALF, 1)
        mode = 2 * jnp.where(row < MODES // 2, row, row - MODES // 2) + parity
        spectra = jnp.where(mode.astype(jnp.float32) <= cutoff, spectra, 0.0)
        sign = -1.0 if parity else 1.0
        spectra = jnp.where(
            slot == HALF - 1,
            (sign * vector_sign) * pltpu.roll(spectra, HALF - 1, 1),
            jnp.where(slot == HALF - 2, sign * pltpu.roll(spectra, HALF - 2 - NEAR, 1), spectra),
        )
        spectra = jnp.concatenate(
            [jnp.where(column < HALF, spectra, 0.0), jnp.where(column < HALF, 0.0, spectra)],
            axis=0,
        )
        high = spectra.astype(jnp.bfloat16)
        rest = spectra - high.astype(jnp.float32)
        medium = rest.astype(jnp.bfloat16)
        low = (rest - medium.astype(jnp.float32)).astype(jnp.bfloat16)
        wide = jnp.concatenate([high, medium], axis=1)
        first = dot(inverse[parity, 0], wide)
        second = dot(inverse[parity, 1], wide)
        third = dot(inverse[parity, 0], low) + dot(inverse[parity, 2], high)
        third = third + second[:, LANES:]
        smooth.append(first[:, :LANES] + (first[:, LANES:] + second[:, :LANES] + third))
    for side in range(2):
        value = smooth[0] - smooth[1] if side else smooth[0] + smooth[1]
        send2[side * pairs : (side + 1) * pairs] = value[: pairs * half].reshape(
            pairs, half, LANES
        )
        for i in range(half):
            first_row = i * sectors + side * pairs
            extra[first_row : first_row + pairs, :] = pltpu.roll(
                value[pairs * half :], (NEAR + QUARTER - SPAN * i) % LANES, 1
            )

    slot8 = jnp.where(lane < HALF, lane, lane - HALF)
    spare = (slot8 >= NEAR + QUARTER) & (slot8 < NEAR + QUARTER + SPAN)

    def edge_lanes(i, carry):
        for d in range(8):
            turned = extra[pl.ds(i * 8 + d, half, stride=sectors), :]
            send2[i * 8 + d] = jnp.where(spare, turned, send2[i * 8 + d])
        return carry

    lax.fori_loop(0, sectors // 8, edge_lanes, 0)
    exchange(send2, recv2, 1, 8 + own_x)

    @pl.when(serves_edge)
    def _():
        side = jnp.where(serves_below, 1, 0)
        neighbour = served + 1 - 2 * side

        def post(peer):
            pltpu.make_async_remote_copy(
                src_ref=send2.at[peer],
                dst_ref=ghost.at[side, own_group],
                send_sem=send_sem.at[6],
                recv_sem=recv_sem.at[6 + side],
                device_id={"az": peer, "ax": neighbour},
                device_id_type=MESH,
            ).start()

        visit(post)

    for copy in edges + far_planes:
        copy.wait_recv()

    def spread(i, carry):
        tile = i // FIELDS
        f = i % FIELDS
        for k in range(planes):
            state[tile, f, k + 1, TOP - 1 : TOP, :] = edge_recv[1, tile, f, k : k + 1, :]
            state[tile, f, k + 1, TOP + theta_dev : TOP + theta_dev + 1, :] = edge_recv[
                0, tile, f, k : k + 1, :
            ]
        return carry

    lax.fori_loop(0, tiles * FIELDS, spread, 0)

    def close(first_tile, last_tile):
        nothing = jnp.zeros((theta_dev, LANES), jnp.float32)
        for plane, edge in ((0, 0), (planes + 1, slabs - 1)):

            @pl.when(slab == edge)
            def _():
                for tile in range(first_tile, last_tile):
                    for f in range(FIELDS):
                        state[tile, f, plane, body, :] = nothing

    close(0, tiles)
    lane_full = lax.broadcasted_iota(jnp.int32, (theta_dev, LANES), 1)

    def advance(tile, k):
        radius = (lane_row + tile * LANES).astype(jnp.float32) + 0.5
        inverse_radius = 1.0 / radius
        inverse_square = 1.0 / (radius * radius)
        spread_rate = time_step * viscosity
        radial_base = (0.5 * spread_rate) * inverse_radius
        theta_rate = (-time_step / (2.0 * step_angle)) * inverse_radius
        theta_spread = (spread_rate / (step_angle * step_angle)) * inverse_square
        turn_rate = time_step * inverse_radius
        swirl = spread_rate * inverse_square
        cross = (spread_rate / step_angle) * inverse_square
        center = [state[tile, f, k + 1, body, :] for f in range(FIELDS)]
        radial = radial_base - (0.5 * time_step) * center[0]
        around = theta_rate * center[1]
        axial = (-0.5 * time_step) * center[2]
        outs = []
        turns = []
        for f in range(FIELDS):
            q = center[f]
            inner = across[f, k] if tile == 0 else state[tile - 1, f, k + 1, body, :]
            outer = 0.0 if tile == tiles - 1 else state[tile + 1, f, k + 1, body, :]
            minus = pltpu.roll(jnp.where(lane_full == LANES - 1, inner, q), 1, 1)
            plus = pltpu.roll(jnp.where(lane_full == 0, outer, q), LANES - 1, 1)
            ahead = state[tile, f, k + 1, pl.ds(TOP + 1, theta_dev), :] - q
            behind = state[tile, f, k + 1, pl.ds(TOP - 1, theta_dev), :] - q
            up = state[tile, f, k + 2, body, :]
            down = state[tile, f, k, body, :]
            turn = ahead - behind
            turns.append(turn)
            out = q + (plus - minus) * radial + turn * around + (up - down) * axial
            out = out + spread_rate * ((plus + minus) + (up + down) - 4.0 * q)
            outs.append(out + theta_spread * (ahead + behind))
        whirl = turn_rate * center[1]
        outs[0] = outs[0] + whirl * center[1] - swirl * center[0] - cross * turns[1]
        outs[1] = outs[1] - whirl * center[0] - swirl * center[1] + cross * turns[0]
        outs[2] = outs[2] + (time_step * buoyancy) * center[3]
        for f in range(FIELDS):
            result[tile, f, k] = outs[f]

    stores = []

    def store(tile, first_plane, count):
        stores.append(
            pltpu.make_async_copy(
                result.at[tile, :, pl.ds(first_plane, count)],
                advanced.at[:, pl.ds(first_plane, count), :, pl.ds(tile * LANES, LANES)],
                store_sem.at[len(stores)],
            )
        )
        stores[-1].start()

    for tile in range(1, tiles):

        def far(k, carry):
            advance(tile, k)
            return carry

        lax.fori_loop(0, planes, far, 0)
        store(tile, 0, planes)

    for copy in far_planes:
        copy.wait_send()
    sublane = lax.broadcasted_iota(jnp.int32, (half, LANES), 0)
    diagonal = (slot8 >= SPAN * sublane) & (slot8 < SPAN * sublane + SPAN)
    low_row = TOP - 1
    high_row = TOP + theta_dev
    is_near = lane < NEAR
    is_near_row = lane_row < NEAR

    def unpack(k):
        tail = state.at[0, 4, k + 1]
        tail0 = tail[TOP:middle, :]
        tail1 = tail[middle : middle + half, :]
        tail2 = tail[low_row : low_row + 1, :]
        tail3 = tail[high_row : high_row + 1, :]
        for f in range(4):
            got = recv2[owner(k, f)]
            turned = pltpu.roll(got, HALF, 1)
            across[f, k, 0:half, :] = turned
            across[f, k, half:, :] = got
            rows = pltpu.roll(got, LANES - NEAR - QUARTER, 1, stride=SPAN, stride_axis=0)
            rows = jnp.sum(jnp.where(diagonal, rows, 0.0), axis=0, keepdims=True)
            here = state.at[0, f, k + 1]
            here[TOP:middle, :] = jnp.where(is_near, got, here[TOP:middle, :])
            here[middle : middle + half, :] = jnp.where(
                is_near, turned, here[middle : middle + half, :]
            )
            here[low_row : low_row + 1, :] = jnp.where(
                is_near_row, rows, here[low_row : low_row + 1, :]
            )
            here[high_row : high_row + 1, :] = jnp.where(
                is_near_row, pltpu.roll(rows, HALF, 1), here[high_row : high_row + 1, :]
            )
            shift = (QUARTER * f - NEAR) % LANES
            other = (shift + HALF) % LANES
            part = (lane >= QUARTER * f) & (lane < QUARTER * (f + 1))
            part_row = (lane_row >= QUARTER * f) & (lane_row < QUARTER * (f + 1))
            tail0 = jnp.where(part, pltpu.roll(got, shift, 1), tail0)
            tail1 = jnp.where(part, pltpu.roll(got, other, 1), tail1)
            tail2 = jnp.where(part_row, pltpu.roll(rows, shift, 1), tail2)
            tail3 = jnp.where(part_row, pltpu.roll(rows, other, 1), tail3)
            if f == 0:
                across[4, k, 0:half, :] = pltpu.roll(got, HALF + 1, 1)
                across[4, k, half:, :] = pltpu.roll(got, 1, 1)
        tail[TOP:middle, :] = tail0
        tail[middle : middle + half, :] = tail1
        tail[low_row : low_row + 1, :] = tail2
        tail[high_row : high_row + 1, :] = tail3

    def unpack_ghost(side, plane):
        tail = state.at[0, 4, plane]
        tail0 = tail[TOP:middle, :]
        tail1 = tail[middle : middle + half, :]
        for f in range(4):
            got = ghost[side, f]
            here = state.at[0, f, plane]
            here[TOP:middle, :] = jnp.where(is_near, got, here[TOP:middle, :])
            here[middle : middle + half, :] = jnp.where(
                is_near, pltpu.roll(got, HALF, 1), here[middle : middle + half, :]
            )
            shift = (QUARTER * f - NEAR) % LANES
            part = (lane >= QUARTER * f) & (lane < QUARTER * (f + 1))
            tail0 = jnp.where(part, pltpu.roll(got, shift, 1), tail0)
            tail1 = jnp.where(part, pltpu.roll(got, (shift + HALF) % LANES, 1), tail1)
        tail[TOP:middle, :] = tail0
        tail[middle : middle + half, :] = tail1

    columns = sectors // 16
    width = planes // columns

    for step in ORDER:
        group_x = (own_x + step) % columns
        whole(recv2, 16, 1, 8 + group_x).wait_recv()

        def unpack_one(i, carry):
            unpack(group_x * width + i)
            return carry

        lax.fori_loop(0, width, unpack_one, 0)

        def inside(i, carry):
            advance(0, group_x * width + i)
            return carry

        lax.fori_loop(1, width - 1, inside, 0)
    for side, plane, edge in ((0, 0, 0), (1, planes + 1, slabs - 1)):

        @pl.when(slab != edge)
        def _():
            whole(ghost.at[side], 4, 6, 6 + side).wait_recv()
            unpack_ghost(side, plane)

    def border(i, carry):
        advance(0, i * width)
        advance(0, i * width + width - 1)
        return carry

    lax.fori_loop(0, columns, border, 0)
    store(0, 0, planes)
    whole(send1, sectors, 0, 0).wait_send()
    whole(send2, sectors, 1, 0).wait_send()

    @pl.when(serves_edge)
    def _():
        whole(send2, sectors, 6, 0).wait_send()

    for copy in edges:
        copy.wait_send()
    for copy in stores:
        copy.wait()


def on_device(fields):
    sectors = lax.axis_size("az")
    slabs = lax.axis_size("ax")
    count, planes, theta_dev, radial = fields.shape
    half = theta_dev // 2
    tiles = radial // LANES
    forward, inverse = transform_tables(sectors, theta_dev)
    hbm = pl.BlockSpec(memory_space=pltpu.HBM)
    return pl.pallas_call(
        functools.partial(stencil_kernel, sectors, slabs),
        out_shape=jax.ShapeDtypeStruct(fields.shape, jnp.float32),
        in_specs=[hbm, hbm, hbm],
        out_specs=hbm,
        scratch_shapes=[
            pltpu.VMEM((tiles, count, planes + 2, theta_dev + 2 * TOP, LANES), jnp.float32),
            pltpu.VMEM((count, planes, theta_dev, LANES), jnp.float32),
            pltpu.VMEM((tiles, count, planes, theta_dev, LANES), jnp.float32),
            pltpu.VMEM(forward.shape, jnp.bfloat16),
            pltpu.VMEM(inverse.shape, jnp.bfloat16),
            pltpu.VMEM((sectors, half, LANES), jnp.float32),
            pltpu.VMEM((sectors, half, LANES), jnp.float32),
            pltpu.VMEM((sectors, half, LANES), jnp.float32),
            pltpu.VMEM((sectors, half, LANES), jnp.float32),
            pltpu.VMEM((sectors * half, LANES), jnp.float32),
            pltpu.VMEM((2, 4, half, LANES), jnp.float32),
            pltpu.VMEM((2, tiles, count, planes, LANES), jnp.float32),
            pltpu.VMEM((2, tiles, count, planes, LANES), jnp.float32),
            pltpu.SemaphoreType.DMA((tiles + 2,)),
            pltpu.SemaphoreType.DMA((tiles + 2,)),
            pltpu.SemaphoreType.DMA((8,)),
            pltpu.SemaphoreType.DMA((12,)),
        ],
        compiler_params=pltpu.CompilerParams(
            collective_id=0, has_side_effects=True, vmem_limit_bytes=48 << 20
        ),
        name="plume_section",
    )(
        pltpu.with_memory_space_constraint(fields, pltpu.HBM),
        pltpu.with_memory_space_constraint(jnp.asarray(forward), pltpu.HBM),
        pltpu.with_memory_space_constraint(jnp.asarray(inverse), pltpu.HBM),
    )


def solution(mesh):
    placed = (P(None, "ax", "az", None),)
    return jax.shard_map(
        on_device, mesh=mesh, in_specs=placed, out_specs=P(None, "ax", "az", None), check_vma=False
    )
```

```python
import functools

import jax
import jax.numpy as jnp
import ml_dtypes
import numpy as np
from jax import lax
from jax.experimental import pallas as pl
from jax.experimental.pallas import tpu as pltpu
from jax.sharding import PartitionSpec as P

NEAR = 40
FIELDS = 5
MODES = 128
LANES = 128
HALF = 64
QUARTER = 10
SPAN = 7
WIDE = 2
WIDE2 = 2
TOP = 8
MESH = pl.DeviceIdType.MESH

viscosity = 0.2
time_step = 0.1
buoyancy = 1.0


def split(table, pieces):
    out = []
    rest = table.astype(np.float32)
    for _ in range(pieces):
        piece = rest.astype(ml_dtypes.bfloat16)
        out.append(piece)
        rest = rest - piece.astype(np.float32)
    return np.stack(out)


def basis(theta, parity, total):
    mode = np.arange(parity, MODES, 2)
    angle = (theta[..., None] * mode % total) * (2.0 * np.pi / total)
    return np.concatenate([np.cos(angle), np.sin(angle)], axis=-1)


def transform_tables(sectors, theta_dev):
    total = sectors * theta_dev
    half = theta_dev // 2
    sector = np.arange(sectors // 2)[:, None] * theta_dev
    forward = []
    inverse = []
    for parity in range(2):
        mode = np.arange(parity, MODES, 2)
        weight = np.concatenate([np.where(mode == 0, 1.0, 2.0), np.full(MODES // 2, 2.0)]) / total
        into = []
        back = []
        for side in range(2):
            theta = (sector + side * half + np.arange(half)).reshape(-1)
            into.append((basis(theta, parity, total) * weight).T)
            edge = sector + (theta_dev if side else -1)
            theta = np.concatenate([theta, edge.reshape(-1)])
            back.append(basis(theta, parity, total))
        forward.append(split(np.concatenate(into, axis=0), 2))
        inverse.append(split(np.concatenate(back, axis=1), 3))
    return np.stack(forward), np.stack(inverse)


def stencil_kernel(
    sectors,
    slabs,
    fields,
    forward_hbm,
    inverse_hbm,
    advanced,
    state,
    across,
    result,
    forward,
    inverse,
    send1,
    recv1,
    send2,
    recv2,
    extra,
    edge_send,
    edge_recv,
    load_sem,
    store_sem,
    send_sem,
    recv_sem,
):
    me = lax.axis_index("az")
    slab = lax.axis_index("ax")
    planes = fields.shape[1]
    theta_dev = fields.shape[2]
    half = theta_dev // 2
    tiles = fields.shape[3] // LANES
    body = pl.ds(TOP, theta_dev)
    middle = TOP + half
    step_angle = 2.0 * np.pi / (sectors * theta_dev)

    loads = []
    for tile in range(tiles):
        loads.append(
            pltpu.make_async_copy(
                fields.at[:, :, :, pl.ds(tile * LANES, LANES)],
                state.at[tile, :, pl.ds(1, planes), body, :],
                load_sem.at[tile],
            )
        )
        loads[-1].start()
    load_forward = pltpu.make_async_copy(forward_hbm, forward, load_sem.at[tiles])
    load_forward.start()
    load_inverse = pltpu.make_async_copy(inverse_hbm, inverse, load_sem.at[tiles + 1])
    load_inverse.start()

    partner = (slab + slabs // 2) % slabs
    above = (slab + 1) % slabs
    below = (slab + slabs - 1) % slabs
    ahead = (me + 1) % sectors
    behind = (me + sectors - 1) % sectors
    own_x = me // 16
    own_y = me // 8 % 2
    own_z = me % 8

    own_group = own_z // 2
    own_plane = me // 8 * 2 + me % 2
    owns_edge = (own_plane == 0) | (own_plane == planes - 1)

    def owner(k, f):
        return k // 2 * 8 + 2 * f + k % 2

    around_x = [(own_x + step) % 4 * 16 for step in range(4)]
    around_y = [(own_y + step) % 2 * 8 for step in range(2)]
    around_z = [(own_z + step) % 8 for step in range(8)]

    def visit(call):
        for step_x in (2, 1, 3, 0):
            for step_z in (4, 3, 5, 2, 6, 1, 7, 0):
                for step_y in range(2):
                    call(around_x[step_x] + around_y[step_y] + around_z[step_z])

    barrier = pltpu.get_barrier_semaphore()

    def greet(peer):
        pl.semaphore_signal(
            barrier, inc=1, device_id={"az": peer, "ax": partner}, device_id_type=MESH
        )

    visit(greet)
    for neighbour in (above, below):
        pl.semaphore_signal(barrier, inc=1, device_id={"ax": neighbour}, device_id_type=MESH)
    for neighbour in (ahead, behind):
        pl.semaphore_signal(barrier, inc=1, device_id={"az": neighbour}, device_id_type=MESH)

    loads[0].wait()
    lane = lax.broadcasted_iota(jnp.int32, (half, LANES), 1)
    lane_row = lax.broadcasted_iota(jnp.int32, (1, LANES), 1)

    def pack(k, carry):
        tail0 = state[0, 4, k + 1, TOP:middle, :]
        tail1 = state[0, 4, k + 1, middle : middle + half, :]
        for f in range(4):
            shift = NEAR - QUARTER * f
            first = jnp.where(
                lane < NEAR, state[0, f, k + 1, TOP:middle, :], pltpu.roll(tail0, shift, 1)
            )
            second = jnp.where(
                lane < NEAR,
                state[0, f, k + 1, middle : middle + half, :],
                pltpu.roll(tail1, shift, 1),
            )
            send1[owner(k, f)] = jnp.where(lane < HALF, first, pltpu.roll(second, HALF, 1))
        return carry

    lax.fori_loop(0, planes, pack, 0)
    pl.semaphore_wait(barrier, sectors + 4)

    def exchange(source, target, index, arrival):
        def post(peer):
            pltpu.make_async_remote_copy(
                src_ref=source.at[peer],
                dst_ref=target.at[me],
                send_sem=send_sem.at[index],
                recv_sem=recv_sem.at[arrival],
                device_id={"az": peer, "ax": partner},
                device_id_type=MESH,
            ).start()

        visit(post)

    def whole(buffer, count, index, arrival):
        return pltpu.make_async_remote_copy(
            src_ref=buffer.at[pl.ds(0, count)],
            dst_ref=buffer.at[pl.ds(0, count)],
            send_sem=send_sem.at[index],
            recv_sem=recv_sem.at[arrival],
            device_id={"az": me, "ax": partner},
            device_id_type=MESH,
        )

    exchange(send1, recv1, 0, 0)

    def plane_copy(first_tile, count, source, target, neighbour, index):
        return pltpu.make_async_remote_copy(
            src_ref=state.at[pl.ds(first_tile, count), :, source, body, :],
            dst_ref=state.at[pl.ds(first_tile, count), :, target, body, :],
            send_sem=send_sem.at[index],
            recv_sem=recv_sem.at[index],
            device_id={"ax": neighbour},
            device_id_type=MESH,
        )

    for load in loads[1:]:
        load.wait()
    far_planes = [
        plane_copy(1, tiles - 1, planes, 0, above, 2),
        plane_copy(1, tiles - 1, 1, planes + 1, below, 3),
    ]
    for copy in far_planes:
        copy.start()

    def collect(i, carry):
        tile = i // FIELDS
        f = i % FIELDS
        for k in range(planes):
            edge_send[0, tile, f, k : k + 1, :] = state[tile, f, k + 1, TOP : TOP + 1, :]
            edge_send[1, tile, f, k : k + 1, :] = state[
                tile, f, k + 1, TOP + theta_dev - 1 : TOP + theta_dev, :
            ]
        return carry

    lax.fori_loop(0, tiles * FIELDS, collect, 0)
    edges = []
    for side, peer in ((0, behind), (1, ahead)):
        edges.append(
            pltpu.make_async_remote_copy(
                src_ref=edge_send.at[side],
                dst_ref=edge_recv.at[side],
                send_sem=send_sem.at[4 + side],
                recv_sem=recv_sem.at[4 + side],
                device_id={"az": peer},
                device_id_type=MESH,
            )
        )
        edges[-1].start()

    load_forward.wait()
    load_inverse.wait()
    whole(recv1, sectors, 0, 0).wait_recv()
    dot = functools.partial(jnp.dot, preferred_element_type=jnp.float32)
    pairs = sectors // 2
    row = lax.broadcasted_iota(jnp.int32, (MODES, LANES), 0)
    column = lax.broadcasted_iota(jnp.int32, (MODES, LANES), 1)
    slot = jnp.where(column < HALF, column, column - HALF)
    group = own_group
    cycle = jnp.where(slot < NEAR, slot, slot - NEAR + QUARTER * group)
    cutoff = jnp.floor((355 * (2 * cycle + 1)).astype(jnp.float32) / 226.0 + 0.001)
    cutoff = jnp.minimum(cutoff, MODES - 1.0)
    vector_sign = jnp.where(group < 2, -1.0, 1.0)
    smooth = []
    for parity in range(2):
        near_half = recv1[0:pairs].reshape(pairs * half, LANES)
        far_half = recv1[pairs:].reshape(pairs * half, LANES)
        values = near_half - far_half if parity else near_half + far_half
        high = values.astype(jnp.bfloat16)
        low = (values - high.astype(jnp.float32)).astype(jnp.bfloat16)
        both = dot(forward[parity, 0], jnp.concatenate([high, low], axis=1))
        spectra = both[:, :LANES] + (both[:, LANES:] + dot(forward[parity, 1], high))
        spectra = jnp.where(column < HALF, spectra[:MODES], spectra[MODES:])
        spectra = spectra + pltpu.roll(spectra, HALF, 1)
        mode = 2 * jnp.where(row < MODES // 2, row, row - MODES // 2) + parity
        spectra = jnp.where(mode.astype(jnp.float32) <= cutoff, spectra, 0.0)
        sign = -1.0 if parity else 1.0
        spectra = jnp.where(
            slot == HALF - 1,
            (sign * vector_sign) * pltpu.roll(spectra, HALF - 1, 1),
            jnp.where(slot == HALF - 2, sign * pltpu.roll(spectra, HALF - 2 - NEAR, 1), spectra),
        )
        spectra = jnp.concatenate(
            [jnp.where(column < HALF, spectra, 0.0), jnp.where(column < HALF, 0.0, spectra)],
            axis=0,
        )
        high = spectra.astype(jnp.bfloat16)
        rest = spectra - high.astype(jnp.float32)
        medium = rest.astype(jnp.bfloat16)
        low = (rest - medium.astype(jnp.float32)).astype(jnp.bfloat16)
        wide = jnp.concatenate([high, medium], axis=1)
        first = dot(inverse[parity, 0], wide)
        second = dot(inverse[parity, 1], wide)
        third = dot(inverse[parity, 0], low) + dot(inverse[parity, 2], high)
        third = third + second[:, LANES:]
        smooth.append(first[:, :LANES] + (first[:, LANES:] + second[:, :LANES] + third))
    for side in range(2):
        value = smooth[0] - smooth[1] if side else smooth[0] + smooth[1]
        send2[side * pairs : (side + 1) * pairs] = value[: pairs * half].reshape(
            pairs, half, LANES
        )
        for i in range(half):
            first_row = i * sectors + side * pairs
            extra[first_row : first_row + pairs, :] = pltpu.roll(
                value[pairs * half :], (NEAR + QUARTER - SPAN * i) % LANES, 1
            )

    slot8 = jnp.where(lane < HALF, lane, lane - HALF)
    spare = (slot8 >= NEAR + QUARTER) & (slot8 < NEAR + QUARTER + SPAN)

    def edge_lanes(i, carry):
        for d in range(8):
            turned = extra[pl.ds(i * 8 + d, half, stride=sectors), :]
            send2[i * 8 + d] = jnp.where(spare, turned, send2[i * 8 + d])
        return carry

    lax.fori_loop(0, sectors // 8, edge_lanes, 0)
    exchange(send2, recv2, 1, jnp.where(owns_edge, 8, 1))

    for copy in edges + far_planes:
        copy.wait_recv()

    def spread(i, carry):
        tile = i // FIELDS
        f = i % FIELDS
        for k in range(planes):
            state[tile, f, k + 1, TOP - 1 : TOP, :] = edge_recv[1, tile, f, k : k + 1, :]
            state[tile, f, k + 1, TOP + theta_dev : TOP + theta_dev + 1, :] = edge_recv[
                0, tile, f, k : k + 1, :
            ]
        return carry

    lax.fori_loop(0, tiles * FIELDS, spread, 0)

    def close(first_tile, last_tile):
        nothing = jnp.zeros((theta_dev, LANES), jnp.float32)
        for plane, edge in ((0, 0), (planes + 1, slabs - 1)):

            @pl.when(slab == edge)
            def _():
                for tile in range(first_tile, last_tile):
                    for f in range(FIELDS):
                        state[tile, f, plane, body, :] = nothing

    close(1, tiles)
    lane_full = lax.broadcasted_iota(jnp.int32, (theta_dev, LANES), 1)

    def advance(tile, k):
        radius = (lane_row + tile * LANES).astype(jnp.float32) + 0.5
        inverse_radius = 1.0 / radius
        inverse_square = 1.0 / (radius * radius)
        spread_rate = time_step * viscosity
        radial_base = (0.5 * spread_rate) * inverse_radius
        theta_rate = (-time_step / (2.0 * step_angle)) * inverse_radius
        theta_spread = (spread_rate / (step_angle * step_angle)) * inverse_square
        turn_rate = time_step * inverse_radius
        swirl = spread_rate * inverse_square
        cross = (spread_rate / step_angle) * inverse_square
        center = [state[tile, f, k + 1, body, :] for f in range(FIELDS)]
        radial = radial_base - (0.5 * time_step) * center[0]
        around = theta_rate * center[1]
        axial = (-0.5 * time_step) * center[2]
        outs = []
        turns = []
        for f in range(FIELDS):
            q = center[f]
            inner = across[f, k] if tile == 0 else state[tile - 1, f, k + 1, body, :]
            outer = 0.0 if tile == tiles - 1 else state[tile + 1, f, k + 1, body, :]
            minus = pltpu.roll(jnp.where(lane_full == LANES - 1, inner, q), 1, 1)
            plus = pltpu.roll(jnp.where(lane_full == 0, outer, q), LANES - 1, 1)
            ahead = state[tile, f, k + 1, pl.ds(TOP + 1, theta_dev), :] - q
            behind = state[tile, f, k + 1, pl.ds(TOP - 1, theta_dev), :] - q
            up = state[tile, f, k + 2, body, :]
            down = state[tile, f, k, body, :]
            turn = ahead - behind
            turns.append(turn)
            out = q + (plus - minus) * radial + turn * around + (up - down) * axial
            out = out + spread_rate * ((plus + minus) + (up + down) - 4.0 * q)
            outs.append(out + theta_spread * (ahead + behind))
        whirl = turn_rate * center[1]
        outs[0] = outs[0] + whirl * center[1] - swirl * center[0] - cross * turns[1]
        outs[1] = outs[1] - whirl * center[0] - swirl * center[1] + cross * turns[0]
        outs[2] = outs[2] + (time_step * buoyancy) * center[3]
        for f in range(FIELDS):
            result[tile, f, k] = outs[f]

    stores = []

    def store(tile, first_plane, count):
        stores.append(
            pltpu.make_async_copy(
                result.at[tile, :, pl.ds(first_plane, count)],
                advanced.at[:, pl.ds(first_plane, count), :, pl.ds(tile * LANES, LANES)],
                store_sem.at[len(stores)],
            )
        )
        stores[-1].start()

    for tile in range(1, tiles):

        def far(k, carry):
            advance(tile, k)
            return carry

        lax.fori_loop(0, planes, far, 0)
        store(tile, 0, planes)

    sublane = lax.broadcasted_iota(jnp.int32, (half, LANES), 0)
    diagonal = (slot8 >= SPAN * sublane) & (slot8 < SPAN * sublane + SPAN)
    low_row = TOP - 1
    high_row = TOP + theta_dev
    is_near = lane < NEAR
    is_near_row = lane_row < NEAR

    def unpack(plane_list):
        updates = []
        for k in plane_list:
            tail = [
                state[0, 4, k + 1, TOP:middle, :],
                state[0, 4, k + 1, middle : middle + half, :],
                state[0, 4, k + 1, low_row : low_row + 1, :],
                state[0, 4, k + 1, high_row : high_row + 1, :],
            ]
            for f in range(4):
                got = recv2[owner(k, f)]
                turned = pltpu.roll(got, HALF, 1)
                rows = pltpu.roll(got, LANES - NEAR - QUARTER, 1, stride=SPAN, stride_axis=0)
                rows = jnp.sum(jnp.where(diagonal, rows, 0.0), axis=0, keepdims=True)
                parts = [
                    jnp.where(is_near, got, state[0, f, k + 1, TOP:middle, :]),
                    jnp.where(is_near, turned, state[0, f, k + 1, middle : middle + half, :]),
                    jnp.where(is_near_row, rows, state[0, f, k + 1, low_row : low_row + 1, :]),
                    jnp.where(
                        is_near_row,
                        pltpu.roll(rows, HALF, 1),
                        state[0, f, k + 1, high_row : high_row + 1, :],
                    ),
                ]
                updates.append((f, k, parts, turned, got))
                shift = (QUARTER * f - NEAR) % LANES
                other = (shift + HALF) % LANES
                part = (lane >= QUARTER * f) & (lane < QUARTER * (f + 1))
                part_row = (lane_row >= QUARTER * f) & (lane_row < QUARTER * (f + 1))
                tail[0] = jnp.where(part, pltpu.roll(got, shift, 1), tail[0])
                tail[1] = jnp.where(part, pltpu.roll(got, other, 1), tail[1])
                tail[2] = jnp.where(part_row, pltpu.roll(rows, shift, 1), tail[2])
                tail[3] = jnp.where(part_row, pltpu.roll(rows, other, 1), tail[3])
                if f == 0:
                    opposite = (pltpu.roll(got, HALF + 1, 1), pltpu.roll(got, 1, 1))
            updates.append((4, k, tail, *opposite))
        for f, k, parts, first, second in updates:
            state[0, f, k + 1, TOP:middle, :] = parts[0]
            state[0, f, k + 1, middle : middle + half, :] = parts[1]
            state[0, f, k + 1, low_row : low_row + 1, :] = parts[2]
            state[0, f, k + 1, high_row : high_row + 1, :] = parts[3]
            across[f, k, 0:half, :] = first
            across[f, k, half:, :] = second

    whole(recv2, 8, 1, 8).wait_recv()
    unpack([0, planes - 1])
    near_planes = [
        plane_copy(0, 1, planes, 0, above, 6),
        plane_copy(0, 1, 1, planes + 1, below, 7),
    ]
    for copy in near_planes:
        copy.start()
    whole(recv2, sectors - 8, 1, 1).wait_recv()

    def unpack_inner(i, carry):
        unpack([1 + i * WIDE + step for step in range(WIDE)])
        return carry

    lax.fori_loop(0, (planes - 2) // WIDE, unpack_inner, 0)

    def near(i, carry):
        for step in range(WIDE2):
            advance(0, 1 + i * WIDE2 + step)
        return carry

    lax.fori_loop(0, (planes - 2) // WIDE2, near, 0)
    store(0, 1, planes - 2)
    for copy in near_planes:
        copy.wait_recv()
    close(0, 1)
    advance(0, 0)
    advance(0, planes - 1)
    store(0, 0, 1)
    store(0, planes - 1, 1)
    whole(send1, sectors, 0, 0).wait_send()
    whole(send2, sectors, 1, 1).wait_send()
    for copy in edges + far_planes + near_planes:
        copy.wait_send()
    for copy in stores:
        copy.wait()


def on_device(fields):
    sectors = lax.axis_size("az")
    slabs = lax.axis_size("ax")
    count, planes, theta_dev, radial = fields.shape
    half = theta_dev // 2
    tiles = radial // LANES
    forward, inverse = transform_tables(sectors, theta_dev)
    hbm = pl.BlockSpec(memory_space=pltpu.HBM)
    return pl.pallas_call(
        functools.partial(stencil_kernel, sectors, slabs),
        out_shape=jax.ShapeDtypeStruct(fields.shape, jnp.float32),
        in_specs=[hbm, hbm, hbm],
        out_specs=hbm,
        scratch_shapes=[
            pltpu.VMEM((tiles, count, planes + 2, theta_dev + 2 * TOP, LANES), jnp.float32),
            pltpu.VMEM((count, planes, theta_dev, LANES), jnp.float32),
            pltpu.VMEM((tiles, count, planes, theta_dev, LANES), jnp.float32),
            pltpu.VMEM(forward.shape, jnp.bfloat16),
            pltpu.VMEM(inverse.shape, jnp.bfloat16),
            pltpu.VMEM((sectors, half, LANES), jnp.float32),
            pltpu.VMEM((sectors, half, LANES), jnp.float32),
            pltpu.VMEM((sectors, half, LANES), jnp.float32),
            pltpu.VMEM((sectors, half, LANES), jnp.float32),
            pltpu.VMEM((sectors * half, LANES), jnp.float32),
            pltpu.VMEM((2, tiles, count, planes, LANES), jnp.float32),
            pltpu.VMEM((2, tiles, count, planes, LANES), jnp.float32),
            pltpu.SemaphoreType.DMA((tiles + 2,)),
            pltpu.SemaphoreType.DMA((tiles + 2,)),
            pltpu.SemaphoreType.DMA((8,)),
            pltpu.SemaphoreType.DMA((9,)),
        ],
        compiler_params=pltpu.CompilerParams(
            collective_id=0, has_side_effects=True, vmem_limit_bytes=48 << 20
        ),
        name="plume_section",
    )(
        pltpu.with_memory_space_constraint(fields, pltpu.HBM),
        pltpu.with_memory_space_constraint(jnp.asarray(forward), pltpu.HBM),
        pltpu.with_memory_space_constraint(jnp.asarray(inverse), pltpu.HBM),
    )


def solution(mesh):
    placed = (P(None, "ax", "az", None),)
    return jax.shard_map(
        on_device, mesh=mesh, in_specs=placed, out_specs=P(None, "ax", "az", None), check_vma=False
    )
```

```python
import functools

import jax
import jax.numpy as jnp
import ml_dtypes
import numpy as np
from jax import lax
from jax.experimental import pallas as pl
from jax.experimental.pallas import tpu as pltpu
from jax.sharding import PartitionSpec as P

NEAR = 40
FIELDS = 5
MODES = 128
LANES = 128
HALF = 64
QUARTER = 10
SPAN = 7
WIDE = 2
WIDE2 = 2
TOP = 8
MESH = pl.DeviceIdType.MESH

viscosity = 0.2
time_step = 0.1
buoyancy = 1.0


def split(table, pieces):
    out = []
    rest = table.astype(np.float32)
    for _ in range(pieces):
        piece = rest.astype(ml_dtypes.bfloat16)
        out.append(piece)
        rest = rest - piece.astype(np.float32)
    return np.stack(out)


def basis(theta, parity, total):
    mode = np.arange(parity, MODES, 2)
    angle = (theta[..., None] * mode % total) * (2.0 * np.pi / total)
    return np.concatenate([np.cos(angle), np.sin(angle)], axis=-1)


def transform_tables(sectors, theta_dev):
    total = sectors * theta_dev
    half = theta_dev // 2
    sector = np.arange(sectors // 2)[:, None] * theta_dev
    forward = []
    inverse = []
    for parity in range(2):
        mode = np.arange(parity, MODES, 2)
        weight = np.concatenate([np.where(mode == 0, 1.0, 2.0), np.full(MODES // 2, 2.0)]) / total
        into = []
        back = []
        for side in range(2):
            theta = (sector + side * half + np.arange(half)).reshape(-1)
            into.append((basis(theta, parity, total) * weight).T)
            edge = sector + (theta_dev if side else -1)
            theta = np.concatenate([theta, edge.reshape(-1)])
            back.append(basis(theta, parity, total))
        forward.append(split(np.concatenate(into, axis=0), 2))
        inverse.append(split(np.concatenate(back, axis=1), 3))
    return np.stack(forward), np.stack(inverse)


def stencil_kernel(
    sectors,
    slabs,
    fields,
    forward_hbm,
    inverse_hbm,
    advanced,
    state,
    across,
    result,
    forward,
    inverse,
    send1,
    recv1,
    send2,
    recv2,
    extra,
    ghost,
    edge_send,
    edge_recv,
    load_sem,
    store_sem,
    send_sem,
    recv_sem,
):
    me = lax.axis_index("az")
    slab = lax.axis_index("ax")
    planes = fields.shape[1]
    theta_dev = fields.shape[2]
    half = theta_dev // 2
    tiles = fields.shape[3] // LANES
    body = pl.ds(TOP, theta_dev)
    middle = TOP + half
    step_angle = 2.0 * np.pi / (sectors * theta_dev)

    loads = []
    for tile in range(tiles):
        loads.append(
            pltpu.make_async_copy(
                fields.at[:, :, :, pl.ds(tile * LANES, LANES)],
                state.at[tile, :, pl.ds(1, planes), body, :],
                load_sem.at[tile],
            )
        )
        loads[-1].start()
    load_forward = pltpu.make_async_copy(forward_hbm, forward, load_sem.at[tiles])
    load_forward.start()
    load_inverse = pltpu.make_async_copy(inverse_hbm, inverse, load_sem.at[tiles + 1])
    load_inverse.start()

    partner = (slab + slabs // 2) % slabs
    above = (slab + 1) % slabs
    below = (slab + slabs - 1) % slabs
    ahead = (me + 1) % sectors
    behind = (me + sectors - 1) % sectors
    own_x = me // 16
    own_y = me // 8 % 2
    own_z = me % 8

    own_group = own_z // 2
    own_plane = me // 8 * 2 + me % 2
    owns_edge = (own_plane == 0) | (own_plane == planes - 1)

    def owner(k, f):
        return k // 2 * 8 + 2 * f + k % 2

    around_x = [(own_x + step) % 4 * 16 for step in range(4)]
    around_y = [(own_y + step) % 2 * 8 for step in range(2)]
    around_z = [(own_z + step) % 8 for step in range(8)]

    def visit(call):
        for step_x in (2, 1, 3, 0):
            for step_z in (4, 0, 3, 1, 5, 7, 2, 6):
                for step_y in range(2):
                    call(around_x[step_x] + around_y[step_y] + around_z[step_z])

    barrier = pltpu.get_barrier_semaphore()

    def greet(peer):
        pl.semaphore_signal(
            barrier, inc=1, device_id={"az": peer, "ax": partner}, device_id_type=MESH
        )

    visit(greet)
    for neighbour in (above, below):
        pl.semaphore_signal(barrier, inc=1, device_id={"ax": neighbour}, device_id_type=MESH)
    for neighbour in (ahead, behind):
        pl.semaphore_signal(barrier, inc=1, device_id={"az": neighbour}, device_id_type=MESH)

    loads[0].wait()
    lane = lax.broadcasted_iota(jnp.int32, (half, LANES), 1)
    lane_row = lax.broadcasted_iota(jnp.int32, (1, LANES), 1)

    def pack(k, carry):
        tail0 = state[0, 4, k + 1, TOP:middle, :]
        tail1 = state[0, 4, k + 1, middle : middle + half, :]
        for f in range(4):
            shift = NEAR - QUARTER * f
            first = jnp.where(
                lane < NEAR, state[0, f, k + 1, TOP:middle, :], pltpu.roll(tail0, shift, 1)
            )
            second = jnp.where(
                lane < NEAR,
                state[0, f, k + 1, middle : middle + half, :],
                pltpu.roll(tail1, shift, 1),
            )
            send1[owner(k, f)] = jnp.where(lane < HALF, first, pltpu.roll(second, HALF, 1))
        return carry

    lax.fori_loop(0, planes, pack, 0)
    pl.semaphore_wait(barrier, sectors + 4)

    def exchange(source, target, index, arrival):
        def post(peer):
            pltpu.make_async_remote_copy(
                src_ref=source.at[peer],
                dst_ref=target.at[me],
                send_sem=send_sem.at[index],
                recv_sem=recv_sem.at[arrival],
                device_id={"az": peer, "ax": partner},
                device_id_type=MESH,
            ).start()

        visit(post)

    def whole(buffer, count, index, arrival):
        return pltpu.make_async_remote_copy(
            src_ref=buffer.at[pl.ds(0, count)],
            dst_ref=buffer.at[pl.ds(0, count)],
            send_sem=send_sem.at[index],
            recv_sem=recv_sem.at[arrival],
            device_id={"az": me, "ax": partner},
            device_id_type=MESH,
        )

    exchange(send1, recv1, 0, 0)

    def plane_copy(first_tile, count, source, target, neighbour, index):
        return pltpu.make_async_remote_copy(
            src_ref=state.at[pl.ds(first_tile, count), :, source, body, :],
            dst_ref=state.at[pl.ds(first_tile, count), :, target, body, :],
            send_sem=send_sem.at[index],
            recv_sem=recv_sem.at[index],
            device_id={"ax": neighbour},
            device_id_type=MESH,
        )

    for load in loads[1:]:
        load.wait()
    far_planes = [
        plane_copy(0, tiles, planes, 0, above, 2),
        plane_copy(0, tiles, 1, planes + 1, below, 3),
    ]
    for copy in far_planes:
        copy.start()

    def collect(i, carry):
        tile = i // FIELDS
        f = i % FIELDS
        for k in range(planes):
            edge_send[0, tile, f, k : k + 1, :] = state[tile, f, k + 1, TOP : TOP + 1, :]
            edge_send[1, tile, f, k : k + 1, :] = state[
                tile, f, k + 1, TOP + theta_dev - 1 : TOP + theta_dev, :
            ]
        return carry

    lax.fori_loop(0, tiles * FIELDS, collect, 0)
    edges = []
    for side, peer in ((0, behind), (1, ahead)):
        edges.append(
            pltpu.make_async_remote_copy(
                src_ref=edge_send.at[side],
                dst_ref=edge_recv.at[side],
                send_sem=send_sem.at[4 + side],
                recv_sem=recv_sem.at[4 + side],
                device_id={"az": peer},
                device_id_type=MESH,
            )
        )
        edges[-1].start()

    load_forward.wait()
    load_inverse.wait()
    whole(recv1, sectors, 0, 0).wait_recv()
    dot = functools.partial(jnp.dot, preferred_element_type=jnp.float32)
    pairs = sectors // 2
    row = lax.broadcasted_iota(jnp.int32, (MODES, LANES), 0)
    column = lax.broadcasted_iota(jnp.int32, (MODES, LANES), 1)
    slot = jnp.where(column < HALF, column, column - HALF)
    group = own_group
    cycle = jnp.where(slot < NEAR, slot, slot - NEAR + QUARTER * group)
    cutoff = jnp.floor((355 * (2 * cycle + 1)).astype(jnp.float32) / 226.0 + 0.001)
    cutoff = jnp.minimum(cutoff, MODES - 1.0)
    vector_sign = jnp.where(group < 2, -1.0, 1.0)
    smooth = []
    for parity in range(2):
        near_half = recv1[0:pairs].reshape(pairs * half, LANES)
        far_half = recv1[pairs:].reshape(pairs * half, LANES)
        values = near_half - far_half if parity else near_half + far_half
        high = values.astype(jnp.bfloat16)
        low = (values - high.astype(jnp.float32)).astype(jnp.bfloat16)
        both = dot(forward[parity, 0], jnp.concatenate([high, low], axis=1))
        spectra = both[:, :LANES] + (both[:, LANES:] + dot(forward[parity, 1], high))
        spectra = jnp.where(column < HALF, spectra[:MODES], spectra[MODES:])
        spectra = spectra + pltpu.roll(spectra, HALF, 1)
        mode = 2 * jnp.where(row < MODES // 2, row, row - MODES // 2) + parity
        spectra = jnp.where(mode.astype(jnp.float32) <= cutoff, spectra, 0.0)
        sign = -1.0 if parity else 1.0
        spectra = jnp.where(
            slot == HALF - 1,
            (sign * vector_sign) * pltpu.roll(spectra, HALF - 1, 1),
            jnp.where(slot == HALF - 2, sign * pltpu.roll(spectra, HALF - 2 - NEAR, 1), spectra),
        )
        spectra = jnp.concatenate(
            [jnp.where(column < HALF, spectra, 0.0), jnp.where(column < HALF, 0.0, spectra)],
            axis=0,
        )
        high = spectra.astype(jnp.bfloat16)
        rest = spectra - high.astype(jnp.float32)
        medium = rest.astype(jnp.bfloat16)
        low = (rest - medium.astype(jnp.float32)).astype(jnp.bfloat16)
        wide = jnp.concatenate([high, medium], axis=1)
        first = dot(inverse[parity, 0], wide)
        second = dot(inverse[parity, 1], wide)
        third = dot(inverse[parity, 0], low) + dot(inverse[parity, 2], high)
        third = third + second[:, LANES:]
        smooth.append(first[:, :LANES] + (first[:, LANES:] + second[:, :LANES] + third))
    for side in range(2):
        value = smooth[0] - smooth[1] if side else smooth[0] + smooth[1]
        send2[side * pairs : (side + 1) * pairs] = value[: pairs * half].reshape(
            pairs, half, LANES
        )
        for i in range(half):
            first_row = i * sectors + side * pairs
            extra[first_row : first_row + pairs, :] = pltpu.roll(
                value[pairs * half :], (NEAR + QUARTER - SPAN * i) % LANES, 1
            )

    slot8 = jnp.where(lane < HALF, lane, lane - HALF)
    spare = (slot8 >= NEAR + QUARTER) & (slot8 < NEAR + QUARTER + SPAN)

    def edge_lanes(i, carry):
        for d in range(8):
            turned = extra[pl.ds(i * 8 + d, half, stride=sectors), :]
            send2[i * 8 + d] = jnp.where(spare, turned, send2[i * 8 + d])
        return carry

    lax.fori_loop(0, sectors // 8, edge_lanes, 0)
    exchange(send2, recv2, 1, jnp.where(owns_edge, 8, 1))

    for copy in edges + far_planes:
        copy.wait_recv()

    def spread(i, carry):
        tile = i // FIELDS
        f = i % FIELDS
        for k in range(planes):
            state[tile, f, k + 1, TOP - 1 : TOP, :] = edge_recv[1, tile, f, k : k + 1, :]
            state[tile, f, k + 1, TOP + theta_dev : TOP + theta_dev + 1, :] = edge_recv[
                0, tile, f, k : k + 1, :
            ]
        return carry

    lax.fori_loop(0, tiles * FIELDS, spread, 0)

    def close(first_tile, last_tile):
        nothing = jnp.zeros((theta_dev, LANES), jnp.float32)
        for plane, edge in ((0, 0), (planes + 1, slabs - 1)):

            @pl.when(slab == edge)
            def _():
                for tile in range(first_tile, last_tile):
                    for f in range(FIELDS):
                        state[tile, f, plane, body, :] = nothing

    close(1, tiles)
    lane_full = lax.broadcasted_iota(jnp.int32, (theta_dev, LANES), 1)

    def advance(tile, k):
        radius = (lane_row + tile * LANES).astype(jnp.float32) + 0.5
        inverse_radius = 1.0 / radius
        inverse_square = 1.0 / (radius * radius)
        spread_rate = time_step * viscosity
        radial_base = (0.5 * spread_rate) * inverse_radius
        theta_rate = (-time_step / (2.0 * step_angle)) * inverse_radius
        theta_spread = (spread_rate / (step_angle * step_angle)) * inverse_square
        turn_rate = time_step * inverse_radius
        swirl = spread_rate * inverse_square
        cross = (spread_rate / step_angle) * inverse_square
        center = [state[tile, f, k + 1, body, :] for f in range(FIELDS)]
        radial = radial_base - (0.5 * time_step) * center[0]
        around = theta_rate * center[1]
        axial = (-0.5 * time_step) * center[2]
        outs = []
        turns = []
        for f in range(FIELDS):
            q = center[f]
            inner = across[f, k] if tile == 0 else state[tile - 1, f, k + 1, body, :]
            outer = 0.0 if tile == tiles - 1 else state[tile + 1, f, k + 1, body, :]
            minus = pltpu.roll(jnp.where(lane_full == LANES - 1, inner, q), 1, 1)
            plus = pltpu.roll(jnp.where(lane_full == 0, outer, q), LANES - 1, 1)
            ahead = state[tile, f, k + 1, pl.ds(TOP + 1, theta_dev), :] - q
            behind = state[tile, f, k + 1, pl.ds(TOP - 1, theta_dev), :] - q
            up = state[tile, f, k + 2, body, :]
            down = state[tile, f, k, body, :]
            turn = ahead - behind
            turns.append(turn)
            out = q + (plus - minus) * radial + turn * around + (up - down) * axial
            out = out + spread_rate * ((plus + minus) + (up + down) - 4.0 * q)
            outs.append(out + theta_spread * (ahead + behind))
        whirl = turn_rate * center[1]
        outs[0] = outs[0] + whirl * center[1] - swirl * center[0] - cross * turns[1]
        outs[1] = outs[1] - whirl * center[0] - swirl * center[1] + cross * turns[0]
        outs[2] = outs[2] + (time_step * buoyancy) * center[3]
        for f in range(FIELDS):
            result[tile, f, k] = outs[f]

    stores = []

    def store(tile, first_plane, count):
        stores.append(
            pltpu.make_async_copy(
                result.at[tile, :, pl.ds(first_plane, count)],
                advanced.at[:, pl.ds(first_plane, count), :, pl.ds(tile * LANES, LANES)],
                store_sem.at[len(stores)],
            )
        )
        stores[-1].start()

    for tile in range(1, tiles):

        def far(k, carry):
            advance(tile, k)
            return carry

        lax.fori_loop(0, planes, far, 0)
        store(tile, 0, planes)

    sublane = lax.broadcasted_iota(jnp.int32, (half, LANES), 0)
    diagonal = (slot8 >= SPAN * sublane) & (slot8 < SPAN * sublane + SPAN)
    low_row = TOP - 1
    high_row = TOP + theta_dev
    is_near = lane < NEAR
    is_near_row = lane_row < NEAR

    def unpack(plane_list):
        updates = []
        for k in plane_list:
            tail = [
                state[0, 4, k + 1, TOP:middle, :],
                state[0, 4, k + 1, middle : middle + half, :],
                state[0, 4, k + 1, low_row : low_row + 1, :],
                state[0, 4, k + 1, high_row : high_row + 1, :],
            ]
            for f in range(4):
                got = recv2[owner(k, f)]
                turned = pltpu.roll(got, HALF, 1)
                rows = pltpu.roll(got, LANES - NEAR - QUARTER, 1, stride=SPAN, stride_axis=0)
                rows = jnp.sum(jnp.where(diagonal, rows, 0.0), axis=0, keepdims=True)
                parts = [
                    jnp.where(is_near, got, state[0, f, k + 1, TOP:middle, :]),
                    jnp.where(is_near, turned, state[0, f, k + 1, middle : middle + half, :]),
                    jnp.where(is_near_row, rows, state[0, f, k + 1, low_row : low_row + 1, :]),
                    jnp.where(
                        is_near_row,
                        pltpu.roll(rows, HALF, 1),
                        state[0, f, k + 1, high_row : high_row + 1, :],
                    ),
                ]
                updates.append((f, k, parts, turned, got))
                shift = (QUARTER * f - NEAR) % LANES
                other = (shift + HALF) % LANES
                part = (lane >= QUARTER * f) & (lane < QUARTER * (f + 1))
                part_row = (lane_row >= QUARTER * f) & (lane_row < QUARTER * (f + 1))
                tail[0] = jnp.where(part, pltpu.roll(got, shift, 1), tail[0])
                tail[1] = jnp.where(part, pltpu.roll(got, other, 1), tail[1])
                tail[2] = jnp.where(part_row, pltpu.roll(rows, shift, 1), tail[2])
                tail[3] = jnp.where(part_row, pltpu.roll(rows, other, 1), tail[3])
                if f == 0:
                    opposite = (pltpu.roll(got, HALF + 1, 1), pltpu.roll(got, 1, 1))
            updates.append((4, k, tail, *opposite))
        for f, k, parts, first, second in updates:
            state[0, f, k + 1, TOP:middle, :] = parts[0]
            state[0, f, k + 1, middle : middle + half, :] = parts[1]
            state[0, f, k + 1, low_row : low_row + 1, :] = parts[2]
            state[0, f, k + 1, high_row : high_row + 1, :] = parts[3]
            across[f, k, 0:half, :] = first
            across[f, k, half:, :] = second

    for copy in far_planes:
        copy.wait_send()

    def unpack_ghosts():
        updates = []
        for side, plane, edge in ((0, 0, 0), (1, planes + 1, slabs - 1)):
            inside = slab != edge
            tail0 = state[0, 4, plane, TOP:middle, :]
            tail1 = state[0, 4, plane, middle : middle + half, :]
            for f in range(4):
                got = ghost[side, f]
                part0 = jnp.where(is_near, got, state[0, f, plane, TOP:middle, :])
                part1 = jnp.where(
                    is_near,
                    pltpu.roll(got, HALF, 1),
                    state[0, f, plane, middle : middle + half, :],
                )
                updates.append((f, plane, inside, part0, part1))
                shift = (QUARTER * f - NEAR) % LANES
                part = (lane >= QUARTER * f) & (lane < QUARTER * (f + 1))
                tail0 = jnp.where(part, pltpu.roll(got, shift, 1), tail0)
                tail1 = jnp.where(part, pltpu.roll(got, (shift + HALF) % LANES, 1), tail1)
            updates.append((4, plane, inside, tail0, tail1))
        for f, plane, inside, part0, part1 in updates:
            state[0, f, plane, TOP:middle, :] = jnp.where(inside, part0, 0.0)
            state[0, f, plane, middle : middle + half, :] = jnp.where(inside, part1, 0.0)

    whole(recv2, 8, 1, 8).wait_recv()
    for f in range(4):
        for side, plane, neighbour in ((0, planes - 1, above), (1, 0, below)):
            pltpu.make_async_remote_copy(
                src_ref=recv2.at[owner(plane, f)],
                dst_ref=ghost.at[side, f],
                send_sem=send_sem.at[6 + side],
                recv_sem=recv_sem.at[6 + side],
                device_id={"ax": neighbour},
                device_id_type=MESH,
            ).start()
    unpack([0, planes - 1])
    whole(recv2, sectors - 8, 1, 1).wait_recv()

    def unpack_inner(i, carry):
        unpack([1 + i * WIDE + step for step in range(WIDE)])
        return carry

    lax.fori_loop(0, (planes - 2) // WIDE, unpack_inner, 0)

    def near(i, carry):
        for step in range(WIDE2):
            advance(0, 1 + i * WIDE2 + step)
        return carry

    lax.fori_loop(0, (planes - 2) // WIDE2, near, 0)
    store(0, 1, planes - 2)
    for side in range(2):
        whole(ghost.at[side], 4, 6 + side, 6 + side).wait_recv()
    unpack_ghosts()
    advance(0, 0)
    advance(0, planes - 1)
    store(0, 0, 1)
    store(0, planes - 1, 1)
    whole(send1, sectors, 0, 0).wait_send()
    whole(send2, sectors, 1, 1).wait_send()
    for side in range(2):
        whole(ghost.at[side], 4, 6 + side, 6 + side).wait_send()
    for copy in edges:
        copy.wait_send()
    for copy in stores:
        copy.wait()


def on_device(fields):
    sectors = lax.axis_size("az")
    slabs = lax.axis_size("ax")
    count, planes, theta_dev, radial = fields.shape
    half = theta_dev // 2
    tiles = radial // LANES
    forward, inverse = transform_tables(sectors, theta_dev)
    hbm = pl.BlockSpec(memory_space=pltpu.HBM)
    return pl.pallas_call(
        functools.partial(stencil_kernel, sectors, slabs),
        out_shape=jax.ShapeDtypeStruct(fields.shape, jnp.float32),
        in_specs=[hbm, hbm, hbm],
        out_specs=hbm,
        scratch_shapes=[
            pltpu.VMEM((tiles, count, planes + 2, theta_dev + 2 * TOP, LANES), jnp.float32),
            pltpu.VMEM((count, planes, theta_dev, LANES), jnp.float32),
            pltpu.VMEM((tiles, count, planes, theta_dev, LANES), jnp.float32),
            pltpu.VMEM(forward.shape, jnp.bfloat16),
            pltpu.VMEM(inverse.shape, jnp.bfloat16),
            pltpu.VMEM((sectors, half, LANES), jnp.float32),
            pltpu.VMEM((sectors, half, LANES), jnp.float32),
            pltpu.VMEM((sectors, half, LANES), jnp.float32),
            pltpu.VMEM((sectors, half, LANES), jnp.float32),
            pltpu.VMEM((sectors * half, LANES), jnp.float32),
            pltpu.VMEM((2, 4, half, LANES), jnp.float32),
            pltpu.VMEM((2, tiles, count, planes, LANES), jnp.float32),
            pltpu.VMEM((2, tiles, count, planes, LANES), jnp.float32),
            pltpu.SemaphoreType.DMA((tiles + 2,)),
            pltpu.SemaphoreType.DMA((tiles + 2,)),
            pltpu.SemaphoreType.DMA((8,)),
            pltpu.SemaphoreType.DMA((9,)),
        ],
        compiler_params=pltpu.CompilerParams(
            collective_id=0, has_side_effects=True, vmem_limit_bytes=48 << 20
        ),
        name="plume_section",
    )(
        pltpu.with_memory_space_constraint(fields, pltpu.HBM),
        pltpu.with_memory_space_constraint(jnp.asarray(forward), pltpu.HBM),
        pltpu.with_memory_space_constraint(jnp.asarray(inverse), pltpu.HBM),
    )


def solution(mesh):
    placed = (P(None, "ax", "az", None),)
    return jax.shard_map(
        on_device, mesh=mesh, in_specs=placed, out_specs=P(None, "ax", "az", None), check_vma=False
    )
```

```python
import functools

import jax
import jax.numpy as jnp
import ml_dtypes
import numpy as np
from jax import lax
from jax.experimental import pallas as pl
from jax.experimental.pallas import tpu as pltpu
from jax.sharding import PartitionSpec as P

NEAR = 40
FIELDS = 5
MODES = 128
LANES = 128
HALF = 64
QUARTER = 10
SPAN = 7
TOP = 8
MESH = pl.DeviceIdType.MESH

viscosity = 0.2
time_step = 0.1
buoyancy = 1.0


def split(table, pieces):
    out = []
    rest = table.astype(np.float32)
    for _ in range(pieces):
        piece = rest.astype(ml_dtypes.bfloat16)
        out.append(piece)
        rest = rest - piece.astype(np.float32)
    return np.stack(out)


def basis(theta, parity, total):
    mode = np.arange(parity, MODES, 2)
    angle = (theta[..., None] * mode % total) * (2.0 * np.pi / total)
    return np.concatenate([np.cos(angle), np.sin(angle)], axis=-1)


def transform_tables(sectors, theta_dev):
    total = sectors * theta_dev
    half = theta_dev // 2
    sector = np.arange(sectors // 2)[:, None] * theta_dev
    forward = []
    inverse = []
    for parity in range(2):
        mode = np.arange(parity, MODES, 2)
        weight = np.concatenate([np.where(mode == 0, 1.0, 2.0), np.full(MODES // 2, 2.0)]) / total
        into = []
        back = []
        for side in range(2):
            theta = (sector + side * half + np.arange(half)).reshape(-1)
            into.append((basis(theta, parity, total) * weight).T)
            edge = sector + (theta_dev if side else -1)
            theta = np.concatenate([theta, edge.reshape(-1)])
            back.append(basis(theta, parity, total))
        forward.append(split(np.concatenate(into, axis=0), 2))
        inverse.append(split(np.concatenate(back, axis=1), 3))
    return np.stack(forward), np.stack(inverse)


def stencil_kernel(
    sectors,
    slabs,
    fields,
    forward_hbm,
    inverse_hbm,
    advanced,
    state,
    across,
    result,
    forward,
    inverse,
    send1,
    recv1,
    send2,
    recv2,
    extra,
    ghost,
    edge_send,
    edge_recv,
    load_sem,
    store_sem,
    send_sem,
    recv_sem,
):
    me = lax.axis_index("az")
    slab = lax.axis_index("ax")
    planes = fields.shape[1]
    theta_dev = fields.shape[2]
    half = theta_dev // 2
    tiles = fields.shape[3] // LANES
    body = pl.ds(TOP, theta_dev)
    middle = TOP + half
    step_angle = 2.0 * np.pi / (sectors * theta_dev)

    loads = []
    for tile in range(tiles):
        loads.append(
            pltpu.make_async_copy(
                fields.at[:, :, :, pl.ds(tile * LANES, LANES)],
                state.at[tile, :, pl.ds(1, planes), body, :],
                load_sem.at[tile],
            )
        )
        loads[-1].start()
    load_forward = pltpu.make_async_copy(forward_hbm, forward, load_sem.at[tiles])
    load_forward.start()
    load_inverse = pltpu.make_async_copy(inverse_hbm, inverse, load_sem.at[tiles + 1])
    load_inverse.start()

    partner = (slab + slabs // 2) % slabs
    above = (slab + 1) % slabs
    below = (slab + slabs - 1) % slabs
    ahead = (me + 1) % sectors
    behind = (me + sectors - 1) % sectors
    own_x = me // 16
    own_y = me // 8 % 2
    own_z = me % 8

    own_group = own_z // 2
    own_plane = me // 8 * 2 + me % 2
    owns_edge = (own_plane == 0) | (own_plane == planes - 1)

    def owner(k, f):
        return k // 2 * 8 + 2 * f + k % 2

    around_x = [(own_x + step) % 4 * 16 for step in range(4)]
    around_y = [(own_y + step) % 2 * 8 for step in range(2)]
    around_z = [(own_z + step) % 8 for step in range(8)]

    def visit(call):
        for step_x in (2, 1, 3, 0):
            for step_z in (4, 0, 3, 1, 5, 7, 2, 6):
                for step_y in range(2):
                    call(around_x[step_x] + around_y[step_y] + around_z[step_z])

    barrier = pltpu.get_barrier_semaphore()

    def greet(peer):
        pl.semaphore_signal(
            barrier, inc=1, device_id={"az": peer, "ax": partner}, device_id_type=MESH
        )

    visit(greet)
    for neighbour in (above, below):
        pl.semaphore_signal(barrier, inc=1, device_id={"ax": neighbour}, device_id_type=MESH)
    for neighbour in (ahead, behind):
        pl.semaphore_signal(barrier, inc=1, device_id={"az": neighbour}, device_id_type=MESH)

    loads[0].wait()
    lane = lax.broadcasted_iota(jnp.int32, (half, LANES), 1)
    lane_row = lax.broadcasted_iota(jnp.int32, (1, LANES), 1)

    def pack(k, carry):
        tail0 = state[0, 4, k + 1, TOP:middle, :]
        tail1 = state[0, 4, k + 1, middle : middle + half, :]
        for f in range(4):
            shift = NEAR - QUARTER * f
            first = jnp.where(
                lane < NEAR, state[0, f, k + 1, TOP:middle, :], pltpu.roll(tail0, shift, 1)
            )
            second = jnp.where(
                lane < NEAR,
                state[0, f, k + 1, middle : middle + half, :],
                pltpu.roll(tail1, shift, 1),
            )
            send1[owner(k, f)] = jnp.where(lane < HALF, first, pltpu.roll(second, HALF, 1))
        return carry

    lax.fori_loop(0, planes, pack, 0)
    pl.semaphore_wait(barrier, sectors + 4)

    def exchange(source, target, index, arrival):
        def post(peer):
            pltpu.make_async_remote_copy(
                src_ref=source.at[peer],
                dst_ref=target.at[me],
                send_sem=send_sem.at[index],
                recv_sem=recv_sem.at[arrival],
                device_id={"az": peer, "ax": partner},
                device_id_type=MESH,
            ).start()

        visit(post)

    def whole(buffer, count, index, arrival):
        return pltpu.make_async_remote_copy(
            src_ref=buffer.at[pl.ds(0, count)],
            dst_ref=buffer.at[pl.ds(0, count)],
            send_sem=send_sem.at[index],
            recv_sem=recv_sem.at[arrival],
            device_id={"az": me, "ax": partner},
            device_id_type=MESH,
        )

    exchange(send1, recv1, 0, 0)

    def plane_copy(first_tile, count, source, target, neighbour, index):
        return pltpu.make_async_remote_copy(
            src_ref=state.at[pl.ds(first_tile, count), :, source, body, :],
            dst_ref=state.at[pl.ds(first_tile, count), :, target, body, :],
            send_sem=send_sem.at[index],
            recv_sem=recv_sem.at[index],
            device_id={"ax": neighbour},
            device_id_type=MESH,
        )

    for load in loads[1:]:
        load.wait()
    far_planes = [
        plane_copy(0, tiles, planes, 0, above, 2),
        plane_copy(0, tiles, 1, planes + 1, below, 3),
    ]
    for copy in far_planes:
        copy.start()

    def collect(i, carry):
        tile = i // FIELDS
        f = i % FIELDS
        for k in range(planes):
            edge_send[0, tile, f, k : k + 1, :] = state[tile, f, k + 1, TOP : TOP + 1, :]
            edge_send[1, tile, f, k : k + 1, :] = state[
                tile, f, k + 1, TOP + theta_dev - 1 : TOP + theta_dev, :
            ]
        return carry

    lax.fori_loop(0, tiles * FIELDS, collect, 0)
    edges = []
    for side, peer in ((0, behind), (1, ahead)):
        edges.append(
            pltpu.make_async_remote_copy(
                src_ref=edge_send.at[side],
                dst_ref=edge_recv.at[side],
                send_sem=send_sem.at[4 + side],
                recv_sem=recv_sem.at[4 + side],
                device_id={"az": peer},
                device_id_type=MESH,
            )
        )
        edges[-1].start()

    load_forward.wait()
    load_inverse.wait()
    whole(recv1, sectors, 0, 0).wait_recv()
    dot = functools.partial(jnp.dot, preferred_element_type=jnp.float32)
    pairs = sectors // 2
    row = lax.broadcasted_iota(jnp.int32, (MODES, LANES), 0)
    column = lax.broadcasted_iota(jnp.int32, (MODES, LANES), 1)
    slot = jnp.where(column < HALF, column, column - HALF)
    group = own_group
    cycle = jnp.where(slot < NEAR, slot, slot - NEAR + QUARTER * group)
    cutoff = jnp.floor((355 * (2 * cycle + 1)).astype(jnp.float32) / 226.0 + 0.001)
    cutoff = jnp.minimum(cutoff, MODES - 1.0)
    vector_sign = jnp.where(group < 2, -1.0, 1.0)
    smooth = []
    for parity in range(2):
        near_half = recv1[0:pairs].reshape(pairs * half, LANES)
        far_half = recv1[pairs:].reshape(pairs * half, LANES)
        values = near_half - far_half if parity else near_half + far_half
        high = values.astype(jnp.bfloat16)
        low = (values - high.astype(jnp.float32)).astype(jnp.bfloat16)
        both = dot(forward[parity, 0], jnp.concatenate([high, low], axis=1))
        spectra = both[:, :LANES] + (both[:, LANES:] + dot(forward[parity, 1], high))
        spectra = jnp.where(column < HALF, spectra[:MODES], spectra[MODES:])
        spectra = spectra + pltpu.roll(spectra, HALF, 1)
        mode = 2 * jnp.where(row < MODES // 2, row, row - MODES // 2) + parity
        spectra = jnp.where(mode.astype(jnp.float32) <= cutoff, spectra, 0.0)
        sign = -1.0 if parity else 1.0
        spectra = jnp.where(
            slot == HALF - 1,
            (sign * vector_sign) * pltpu.roll(spectra, HALF - 1, 1),
            jnp.where(slot == HALF - 2, sign * pltpu.roll(spectra, HALF - 2 - NEAR, 1), spectra),
        )
        spectra = jnp.concatenate(
            [jnp.where(column < HALF, spectra, 0.0), jnp.where(column < HALF, 0.0, spectra)],
            axis=0,
        )
        high = spectra.astype(jnp.bfloat16)
        rest = spectra - high.astype(jnp.float32)
        medium = rest.astype(jnp.bfloat16)
        low = (rest - medium.astype(jnp.float32)).astype(jnp.bfloat16)
        wide = jnp.concatenate([high, medium], axis=1)
        first = dot(inverse[parity, 0], wide)
        second = dot(inverse[parity, 1], wide)
        third = dot(inverse[parity, 0], low) + dot(inverse[parity, 2], high)
        third = third + second[:, LANES:]
        smooth.append(first[:, :LANES] + (first[:, LANES:] + second[:, :LANES] + third))
    for side in range(2):
        value = smooth[0] - smooth[1] if side else smooth[0] + smooth[1]
        send2[side * pairs : (side + 1) * pairs] = value[: pairs * half].reshape(
            pairs, half, LANES
        )
        for i in range(half):
            first_row = i * sectors + side * pairs
            extra[first_row : first_row + pairs, :] = pltpu.roll(
                value[pairs * half :], (NEAR + QUARTER - SPAN * i) % LANES, 1
            )

    slot8 = jnp.where(lane < HALF, lane, lane - HALF)
    spare = (slot8 >= NEAR + QUARTER) & (slot8 < NEAR + QUARTER + SPAN)

    def edge_lanes(i, carry):
        for d in range(8):
            turned = extra[pl.ds(i * 8 + d, half, stride=sectors), :]
            send2[i * 8 + d] = jnp.where(spare, turned, send2[i * 8 + d])
        return carry

    lax.fori_loop(0, sectors // 8, edge_lanes, 0)
    exchange(send2, recv2, 1, jnp.where(owns_edge, 8, 1))

    for copy in edges + far_planes:
        copy.wait_recv()

    def spread(i, carry):
        tile = i // FIELDS
        f = i % FIELDS
        for k in range(planes):
            state[tile, f, k + 1, TOP - 1 : TOP, :] = edge_recv[1, tile, f, k : k + 1, :]
            state[tile, f, k + 1, TOP + theta_dev : TOP + theta_dev + 1, :] = edge_recv[
                0, tile, f, k : k + 1, :
            ]
        return carry

    lax.fori_loop(0, tiles * FIELDS, spread, 0)

    def close(first_tile, last_tile):
        nothing = jnp.zeros((theta_dev, LANES), jnp.float32)
        for plane, edge in ((0, 0), (planes + 1, slabs - 1)):

            @pl.when(slab == edge)
            def _():
                for tile in range(first_tile, last_tile):
                    for f in range(FIELDS):
                        state[tile, f, plane, body, :] = nothing

    close(1, tiles)
    lane_full = lax.broadcasted_iota(jnp.int32, (theta_dev, LANES), 1)
    for copy in far_planes:
        copy.wait_send()
    for plane, edge in ((0, 0), (planes + 1, slabs - 1)):
        for f in range(FIELDS):
            known = (lane_full >= NEAR) & (slab != edge)
            state[0, f, plane, body, :] = jnp.where(known, state[0, f, plane, body, :], 0.0)

    def advance(tile, k):
        radius = (lane_row + tile * LANES).astype(jnp.float32) + 0.5
        inverse_radius = 1.0 / radius
        inverse_square = 1.0 / (radius * radius)
        spread_rate = time_step * viscosity
        radial_base = (0.5 * spread_rate) * inverse_radius
        theta_rate = (-time_step / (2.0 * step_angle)) * inverse_radius
        theta_spread = (spread_rate / (step_angle * step_angle)) * inverse_square
        turn_rate = time_step * inverse_radius
        swirl = spread_rate * inverse_square
        cross = (spread_rate / step_angle) * inverse_square
        center = [state[tile, f, k + 1, body, :] for f in range(FIELDS)]
        radial = radial_base - (0.5 * time_step) * center[0]
        around = theta_rate * center[1]
        axial = (-0.5 * time_step) * center[2]
        outs = []
        turns = []
        for f in range(FIELDS):
            q = center[f]
            inner = across[f, k] if tile == 0 else state[tile - 1, f, k + 1, body, :]
            outer = 0.0 if tile == tiles - 1 else state[tile + 1, f, k + 1, body, :]
            minus = pltpu.roll(jnp.where(lane_full == LANES - 1, inner, q), 1, 1)
            plus = pltpu.roll(jnp.where(lane_full == 0, outer, q), LANES - 1, 1)
            ahead = state[tile, f, k + 1, pl.ds(TOP + 1, theta_dev), :] - q
            behind = state[tile, f, k + 1, pl.ds(TOP - 1, theta_dev), :] - q
            up = state[tile, f, k + 2, body, :]
            down = state[tile, f, k, body, :]
            turn = ahead - behind
            turns.append(turn)
            out = q + (plus - minus) * radial + turn * around + (up - down) * axial
            out = out + spread_rate * ((plus + minus) + (up + down) - 4.0 * q)
            outs.append(out + theta_spread * (ahead + behind))
        whirl = turn_rate * center[1]
        outs[0] = outs[0] + whirl * center[1] - swirl * center[0] - cross * turns[1]
        outs[1] = outs[1] - whirl * center[0] - swirl * center[1] + cross * turns[0]
        outs[2] = outs[2] + (time_step * buoyancy) * center[3]
        for f in range(FIELDS):
            result[tile, f, k] = outs[f]

    stores = []

    def store(tile, first_plane, count):
        stores.append(
            pltpu.make_async_copy(
                result.at[tile, :, pl.ds(first_plane, count)],
                advanced.at[:, pl.ds(first_plane, count), :, pl.ds(tile * LANES, LANES)],
                store_sem.at[len(stores)],
            )
        )
        stores[-1].start()

    for tile in range(1, tiles):

        def far(k, carry):
            advance(tile, k)
            return carry

        lax.fori_loop(0, planes, far, 0)
        store(tile, 0, planes)

    sublane = lax.broadcasted_iota(jnp.int32, (half, LANES), 0)
    diagonal = (slot8 >= SPAN * sublane) & (slot8 < SPAN * sublane + SPAN)
    low_row = TOP - 1
    high_row = TOP + theta_dev
    is_near = lane < NEAR
    is_near_row = lane_row < NEAR

    def unpack(plane_list):
        updates = []
        for k in plane_list:
            tail = [
                state[0, 4, k + 1, TOP:middle, :],
                state[0, 4, k + 1, middle : middle + half, :],
                state[0, 4, k + 1, low_row : low_row + 1, :],
                state[0, 4, k + 1, high_row : high_row + 1, :],
            ]
            for f in range(4):
                got = recv2[owner(k, f)]
                turned = pltpu.roll(got, HALF, 1)
                rows = pltpu.roll(got, LANES - NEAR - QUARTER, 1, stride=SPAN, stride_axis=0)
                rows = jnp.sum(jnp.where(diagonal, rows, 0.0), axis=0, keepdims=True)
                parts = [
                    jnp.where(is_near, got, state[0, f, k + 1, TOP:middle, :]),
                    jnp.where(is_near, turned, state[0, f, k + 1, middle : middle + half, :]),
                    jnp.where(is_near_row, rows, state[0, f, k + 1, low_row : low_row + 1, :]),
                    jnp.where(
                        is_near_row,
                        pltpu.roll(rows, HALF, 1),
                        state[0, f, k + 1, high_row : high_row + 1, :],
                    ),
                ]
                updates.append((f, k, parts, turned, got))
                shift = (QUARTER * f - NEAR) % LANES
                other = (shift + HALF) % LANES
                part = (lane >= QUARTER * f) & (lane < QUARTER * (f + 1))
                part_row = (lane_row >= QUARTER * f) & (lane_row < QUARTER * (f + 1))
                tail[0] = jnp.where(part, pltpu.roll(got, shift, 1), tail[0])
                tail[1] = jnp.where(part, pltpu.roll(got, other, 1), tail[1])
                tail[2] = jnp.where(part_row, pltpu.roll(rows, shift, 1), tail[2])
                tail[3] = jnp.where(part_row, pltpu.roll(rows, other, 1), tail[3])
                if f == 0:
                    opposite = (pltpu.roll(got, HALF + 1, 1), pltpu.roll(got, 1, 1))
            updates.append((4, k, tail, *opposite))
        for f, k, parts, first, second in updates:
            state[0, f, k + 1, TOP:middle, :] = parts[0]
            state[0, f, k + 1, middle : middle + half, :] = parts[1]
            state[0, f, k + 1, low_row : low_row + 1, :] = parts[2]
            state[0, f, k + 1, high_row : high_row + 1, :] = parts[3]
            across[f, k, 0:half, :] = first
            across[f, k, half:, :] = second

    def add_ghosts():
        updates = []
        spread_rate = time_step * viscosity
        for side, k, edge in ((0, 0, 0), (1, planes - 1, slabs - 1)):
            sign = 0.5 * time_step * (1 - 2 * side)
            inside = is_near & (slab != edge)
            rate0 = spread_rate + sign * state[0, 2, k + 1, TOP:middle, :]
            rate1 = spread_rate + sign * state[0, 2, k + 1, middle : middle + half, :]
            tail0 = jnp.zeros((half, LANES), jnp.float32)
            tail1 = tail0
            parts = []
            for f in range(4):
                got = ghost[side, f]
                parts.append((f, got, pltpu.roll(got, HALF, 1)))
                shift = (QUARTER * f - NEAR) % LANES
                part = (lane >= QUARTER * f) & (lane < QUARTER * (f + 1))
                tail0 = jnp.where(part, pltpu.roll(got, shift, 1), tail0)
                tail1 = jnp.where(part, pltpu.roll(got, (shift + HALF) % LANES, 1), tail1)
            parts.append((4, tail0, tail1))
            for f, part0, part1 in parts:
                updates.append(
                    (
                        f,
                        k,
                        result[0, f, k, :half, :] + jnp.where(inside, part0 * rate0, 0.0),
                        result[0, f, k, half:, :] + jnp.where(inside, part1 * rate1, 0.0),
                    )
                )
        for f, k, part0, part1 in updates:
            result[0, f, k, :half, :] = part0
            result[0, f, k, half:, :] = part1

    whole(recv2, 8, 1, 8).wait_recv()
    for f in range(4):
        for side, plane, neighbour in ((0, planes - 1, above), (1, 0, below)):
            pltpu.make_async_remote_copy(
                src_ref=recv2.at[owner(plane, f)],
                dst_ref=ghost.at[side, f],
                send_sem=send_sem.at[6 + side],
                recv_sem=recv_sem.at[6 + side],
                device_id={"ax": neighbour},
                device_id_type=MESH,
            ).start()
    unpack([0, planes - 1])
    whole(recv2, sectors - 8, 1, 1).wait_recv()

    unpack([1, 2])

    def near(i, carry):
        advance(0, 2 * i - 2)
        advance(0, 2 * i - 1)
        unpack([2 * i + 1, 2 * i + 2])
        return carry

    lax.fori_loop(1, planes // 2 - 1, near, 0)
    store(0, 1, planes - 5)
    for k in range(planes - 4, planes):
        advance(0, k)
    store(0, planes - 4, 3)
    for side in range(2):
        whole(ghost.at[side], 4, 6 + side, 6 + side).wait_recv()
    add_ghosts()
    store(0, 0, 1)
    store(0, planes - 1, 1)
    whole(send1, sectors, 0, 0).wait_send()
    whole(send2, sectors, 1, 1).wait_send()
    for side in range(2):
        whole(ghost.at[side], 4, 6 + side, 6 + side).wait_send()
    for copy in edges:
        copy.wait_send()
    for copy in stores:
        copy.wait()


def on_device(fields):
    sectors = lax.axis_size("az")
    slabs = lax.axis_size("ax")
    count, planes, theta_dev, radial = fields.shape
    half = theta_dev // 2
    tiles = radial // LANES
    forward, inverse = transform_tables(sectors, theta_dev)
    hbm = pl.BlockSpec(memory_space=pltpu.HBM)
    return pl.pallas_call(
        functools.partial(stencil_kernel, sectors, slabs),
        out_shape=jax.ShapeDtypeStruct(fields.shape, jnp.float32),
        in_specs=[hbm, hbm, hbm],
        out_specs=hbm,
        scratch_shapes=[
            pltpu.VMEM((tiles, count, planes + 2, theta_dev + 2 * TOP, LANES), jnp.float32),
            pltpu.VMEM((count, planes, theta_dev, LANES), jnp.float32),
            pltpu.VMEM((tiles, count, planes, theta_dev, LANES), jnp.float32),
            pltpu.VMEM(forward.shape, jnp.bfloat16),
            pltpu.VMEM(inverse.shape, jnp.bfloat16),
            pltpu.VMEM((sectors, half, LANES), jnp.float32),
            pltpu.VMEM((sectors, half, LANES), jnp.float32),
            pltpu.VMEM((sectors, half, LANES), jnp.float32),
            pltpu.VMEM((sectors, half, LANES), jnp.float32),
            pltpu.VMEM((sectors * half, LANES), jnp.float32),
            pltpu.VMEM((2, 4, half, LANES), jnp.float32),
            pltpu.VMEM((2, tiles, count, planes, LANES), jnp.float32),
            pltpu.VMEM((2, tiles, count, planes, LANES), jnp.float32),
            pltpu.SemaphoreType.DMA((tiles + 2,)),
            pltpu.SemaphoreType.DMA((tiles + 3,)),
            pltpu.SemaphoreType.DMA((8,)),
            pltpu.SemaphoreType.DMA((9,)),
        ],
        compiler_params=pltpu.CompilerParams(
            collective_id=0, has_side_effects=True, vmem_limit_bytes=48 << 20
        ),
        name="plume_section",
    )(
        pltpu.with_memory_space_constraint(fields, pltpu.HBM),
        pltpu.with_memory_space_constraint(jnp.asarray(forward), pltpu.HBM),
        pltpu.with_memory_space_constraint(jnp.asarray(inverse), pltpu.HBM),
    )


def solution(mesh):
    placed = (P(None, "ax", "az", None),)
    return jax.shard_map(
        on_device, mesh=mesh, in_specs=placed, out_specs=P(None, "ax", "az", None), check_vma=False
    )
```

```python
import functools

import jax
import jax.numpy as jnp
import ml_dtypes
import numpy as np
from jax import lax
from jax.experimental import pallas as pl
from jax.experimental.pallas import tpu as pltpu
from jax.sharding import PartitionSpec as P

NEAR = 40
FIELDS = 5
MODES = 128
LANES = 128
HALF = 64
QUARTER = 10
SPAN = 7
WIDE = 2
WIDE2 = 2
TOP = 8
MESH = pl.DeviceIdType.MESH

viscosity = 0.2
time_step = 0.1
buoyancy = 1.0


def split(table, pieces):
    out = []
    rest = table.astype(np.float32)
    for _ in range(pieces):
        piece = rest.astype(ml_dtypes.bfloat16)
        out.append(piece)
        rest = rest - piece.astype(np.float32)
    return np.stack(out)


def basis(theta, parity, total):
    mode = np.arange(parity, MODES, 2)
    angle = (theta[..., None] * mode % total) * (2.0 * np.pi / total)
    return np.concatenate([np.cos(angle), np.sin(angle)], axis=-1)


def transform_tables(sectors, theta_dev):
    total = sectors * theta_dev
    half = theta_dev // 2
    sector = np.arange(sectors // 2)[:, None] * theta_dev
    forward = []
    inverse = []
    for parity in range(2):
        mode = np.arange(parity, MODES, 2)
        weight = np.concatenate([np.where(mode == 0, 1.0, 2.0), np.full(MODES // 2, 2.0)]) / total
        into = []
        back = []
        for side in range(2):
            theta = (sector + side * half + np.arange(half)).reshape(-1)
            into.append((basis(theta, parity, total) * weight).T)
            edge = sector + (theta_dev if side else -1)
            theta = np.concatenate([theta, edge.reshape(-1)])
            back.append(basis(theta, parity, total))
        forward.append(split(np.concatenate(into, axis=0), 2))
        inverse.append(split(np.concatenate(back, axis=1), 3))
    return np.stack(forward), np.stack(inverse)


def stencil_kernel(
    sectors,
    slabs,
    fields,
    forward_hbm,
    inverse_hbm,
    advanced,
    state,
    across,
    result,
    forward,
    inverse,
    send1,
    recv1,
    send2,
    recv2,
    extra,
    ghost,
    edge_send,
    edge_recv,
    load_sem,
    store_sem,
    send_sem,
    recv_sem,
):
    me = lax.axis_index("az")
    slab = lax.axis_index("ax")
    planes = fields.shape[1]
    theta_dev = fields.shape[2]
    half = theta_dev // 2
    tiles = fields.shape[3] // LANES
    body = pl.ds(TOP, theta_dev)
    middle = TOP + half
    step_angle = 2.0 * np.pi / (sectors * theta_dev)

    loads = []
    for tile in range(tiles):
        loads.append(
            pltpu.make_async_copy(
                fields.at[:, :, :, pl.ds(tile * LANES, LANES)],
                state.at[tile, :, pl.ds(1, planes), body, :],
                load_sem.at[tile],
            )
        )
        loads[-1].start()
    load_forward = pltpu.make_async_copy(forward_hbm, forward, load_sem.at[tiles])
    load_forward.start()
    load_inverse = pltpu.make_async_copy(inverse_hbm, inverse, load_sem.at[tiles + 1])
    load_inverse.start()

    partner = (slab + slabs // 2) % slabs
    above = (slab + 1) % slabs
    below = (slab + slabs - 1) % slabs
    ahead = (me + 1) % sectors
    behind = (me + sectors - 1) % sectors
    own_x = me // 16
    own_y = me // 8 % 2
    own_z = me % 8

    own_group = own_z // 2
    own_plane = me // 8 * 2 + me % 2
    owns_edge = (own_plane == 0) | (own_plane == planes - 1)

    def owner(k, f):
        return k // 2 * 8 + 2 * f + k % 2

    around_x = [(own_x + step) % 4 * 16 for step in range(4)]
    around_y = [(own_y + step) % 2 * 8 for step in range(2)]
    around_z = [(own_z + step) % 8 for step in range(8)]

    def visit(call):
        for step_x in (2, 3, 1, 0):
            for step_z in (4, 7, 3, 1, 5, 0, 2, 6):
                for step_y in range(2):
                    call(around_x[step_x] + around_y[step_y] + around_z[step_z])

    barrier = pltpu.get_barrier_semaphore()

    def greet(peer):
        pl.semaphore_signal(
            barrier, inc=1, device_id={"az": peer, "ax": partner}, device_id_type=MESH
        )

    visit(greet)
    for neighbour in (above, below):
        pl.semaphore_signal(barrier, inc=1, device_id={"ax": neighbour}, device_id_type=MESH)
    for neighbour in (ahead, behind):
        pl.semaphore_signal(barrier, inc=1, device_id={"az": neighbour}, device_id_type=MESH)

    loads[0].wait()
    lane = lax.broadcasted_iota(jnp.int32, (half, LANES), 1)
    lane_row = lax.broadcasted_iota(jnp.int32, (1, LANES), 1)

    def pack(k, carry):
        tail0 = state[0, 4, k + 1, TOP:middle, :]
        tail1 = state[0, 4, k + 1, middle : middle + half, :]
        for f in range(4):
            shift = NEAR - QUARTER * f
            first = jnp.where(
                lane < NEAR, state[0, f, k + 1, TOP:middle, :], pltpu.roll(tail0, shift, 1)
            )
            second = jnp.where(
                lane < NEAR,
                state[0, f, k + 1, middle : middle + half, :],
                pltpu.roll(tail1, shift, 1),
            )
            send1[owner(k, f)] = jnp.where(lane < HALF, first, pltpu.roll(second, HALF, 1))
        return carry

    lax.fori_loop(0, planes, pack, 0)
    pl.semaphore_wait(barrier, sectors + 4)

    def exchange(source, target, index, arrival):
        def post(peer):
            pltpu.make_async_remote_copy(
                src_ref=source.at[peer],
                dst_ref=target.at[me],
                send_sem=send_sem.at[index],
                recv_sem=recv_sem.at[arrival],
                device_id={"az": peer, "ax": partner},
                device_id_type=MESH,
            ).start()

        visit(post)

    def whole(buffer, count, index, arrival):
        return pltpu.make_async_remote_copy(
            src_ref=buffer.at[pl.ds(0, count)],
            dst_ref=buffer.at[pl.ds(0, count)],
            send_sem=send_sem.at[index],
            recv_sem=recv_sem.at[arrival],
            device_id={"az": me, "ax": partner},
            device_id_type=MESH,
        )

    exchange(send1, recv1, 0, 0)

    def plane_copy(first_tile, count, source, target, neighbour, index):
        return pltpu.make_async_remote_copy(
            src_ref=state.at[pl.ds(first_tile, count), :, source, body, :],
            dst_ref=state.at[pl.ds(first_tile, count), :, target, body, :],
            send_sem=send_sem.at[index],
            recv_sem=recv_sem.at[index],
            device_id={"ax": neighbour},
            device_id_type=MESH,
        )

    for load in loads[1:]:
        load.wait()
    far_planes = [
        plane_copy(0, tiles, planes, 0, above, 2),
        plane_copy(0, tiles, 1, planes + 1, below, 3),
    ]
    for copy in far_planes:
        copy.start()

    def collect(i, carry):
        tile = i // FIELDS
        f = i % FIELDS
        for k in range(planes):
            edge_send[0, tile, f, k : k + 1, :] = state[tile, f, k + 1, TOP : TOP + 1, :]
            edge_send[1, tile, f, k : k + 1, :] = state[
                tile, f, k + 1, TOP + theta_dev - 1 : TOP + theta_dev, :
            ]
        return carry

    lax.fori_loop(0, tiles * FIELDS, collect, 0)
    edges = []
    for side, peer in ((0, behind), (1, ahead)):
        edges.append(
            pltpu.make_async_remote_copy(
                src_ref=edge_send.at[side],
                dst_ref=edge_recv.at[side],
                send_sem=send_sem.at[4 + side],
                recv_sem=recv_sem.at[4 + side],
                device_id={"az": peer},
                device_id_type=MESH,
            )
        )
        edges[-1].start()

    load_forward.wait()
    load_inverse.wait()
    whole(recv1, sectors, 0, 0).wait_recv()
    dot = functools.partial(jnp.dot, preferred_element_type=jnp.float32)
    pairs = sectors // 2
    row = lax.broadcasted_iota(jnp.int32, (MODES, LANES), 0)
    column = lax.broadcasted_iota(jnp.int32, (MODES, LANES), 1)
    slot = jnp.where(column < HALF, column, column - HALF)
    group = own_group
    cycle = jnp.where(slot < NEAR, slot, slot - NEAR + QUARTER * group)
    cutoff = jnp.floor((355 * (2 * cycle + 1)).astype(jnp.float32) / 226.0 + 0.001)
    cutoff = jnp.minimum(cutoff, MODES - 1.0)
    vector_sign = jnp.where(group < 2, -1.0, 1.0)
    smooth = []
    for parity in range(2):
        near_half = recv1[0:pairs].reshape(pairs * half, LANES)
        far_half = recv1[pairs:].reshape(pairs * half, LANES)
        values = near_half - far_half if parity else near_half + far_half
        high = values.astype(jnp.bfloat16)
        low = (values - high.astype(jnp.float32)).astype(jnp.bfloat16)
        both = dot(forward[parity, 0], jnp.concatenate([high, low], axis=1))
        spectra = both[:, :LANES] + (both[:, LANES:] + dot(forward[parity, 1], high))
        spectra = jnp.where(column < HALF, spectra[:MODES], spectra[MODES:])
        spectra = spectra + pltpu.roll(spectra, HALF, 1)
        mode = 2 * jnp.where(row < MODES // 2, row, row - MODES // 2) + parity
        spectra = jnp.where(mode.astype(jnp.float32) <= cutoff, spectra, 0.0)
        sign = -1.0 if parity else 1.0
        spectra = jnp.where(
            slot == HALF - 1,
            (sign * vector_sign) * pltpu.roll(spectra, HALF - 1, 1),
            jnp.where(slot == HALF - 2, sign * pltpu.roll(spectra, HALF - 2 - NEAR, 1), spectra),
        )
        spectra = jnp.concatenate(
            [jnp.where(column < HALF, spectra, 0.0), jnp.where(column < HALF, 0.0, spectra)],
            axis=0,
        )
        high = spectra.astype(jnp.bfloat16)
        rest = spectra - high.astype(jnp.float32)
        medium = rest.astype(jnp.bfloat16)
        low = (rest - medium.astype(jnp.float32)).astype(jnp.bfloat16)
        wide = jnp.concatenate([high, medium], axis=1)
        first = dot(inverse[parity, 0], wide)
        second = dot(inverse[parity, 1], wide)
        third = dot(inverse[parity, 0], low) + dot(inverse[parity, 2], high)
        third = third + second[:, LANES:]
        smooth.append(first[:, :LANES] + (first[:, LANES:] + second[:, :LANES] + third))
    for side in range(2):
        value = smooth[0] - smooth[1] if side else smooth[0] + smooth[1]
        send2[side * pairs : (side + 1) * pairs] = value[: pairs * half].reshape(
            pairs, half, LANES
        )
        for i in range(half):
            first_row = i * sectors + side * pairs
            extra[first_row : first_row + pairs, :] = pltpu.roll(
                value[pairs * half :], (NEAR + QUARTER - SPAN * i) % LANES, 1
            )

    slot8 = jnp.where(lane < HALF, lane, lane - HALF)
    spare = (slot8 >= NEAR + QUARTER) & (slot8 < NEAR + QUARTER + SPAN)

    def edge_lanes(i, carry):
        for d in range(8):
            turned = extra[pl.ds(i * 8 + d, half, stride=sectors), :]
            send2[i * 8 + d] = jnp.where(spare, turned, send2[i * 8 + d])
        return carry

    lax.fori_loop(0, sectors // 8, edge_lanes, 0)
    exchange(send2, recv2, 1, jnp.where(owns_edge, 8, 1))

    for copy in edges + far_planes:
        copy.wait_recv()

    def spread(i, carry):
        tile = i // FIELDS
        f = i % FIELDS
        for k in range(planes):
            state[tile, f, k + 1, TOP - 1 : TOP, :] = edge_recv[1, tile, f, k : k + 1, :]
            state[tile, f, k + 1, TOP + theta_dev : TOP + theta_dev + 1, :] = edge_recv[
                0, tile, f, k : k + 1, :
            ]
        return carry

    lax.fori_loop(0, tiles * FIELDS, spread, 0)

    def close(first_tile, last_tile):
        nothing = jnp.zeros((theta_dev, LANES), jnp.float32)
        for plane, edge in ((0, 0), (planes + 1, slabs - 1)):

            @pl.when(slab == edge)
            def _():
                for tile in range(first_tile, last_tile):
                    for f in range(FIELDS):
                        state[tile, f, plane, body, :] = nothing

    close(1, tiles)
    lane_full = lax.broadcasted_iota(jnp.int32, (theta_dev, LANES), 1)

    def advance(tile, k):
        radius = (lane_row + tile * LANES).astype(jnp.float32) + 0.5
        inverse_radius = 1.0 / radius
        inverse_square = 1.0 / (radius * radius)
        spread_rate = time_step * viscosity
        radial_base = (0.5 * spread_rate) * inverse_radius
        theta_rate = (-time_step / (2.0 * step_angle)) * inverse_radius
        theta_spread = (spread_rate / (step_angle * step_angle)) * inverse_square
        turn_rate = time_step * inverse_radius
        swirl = spread_rate * inverse_square
        cross = (spread_rate / step_angle) * inverse_square
        center = [state[tile, f, k + 1, body, :] for f in range(FIELDS)]
        radial = radial_base - (0.5 * time_step) * center[0]
        around = theta_rate * center[1]
        axial = (-0.5 * time_step) * center[2]
        outs = []
        turns = []
        for f in range(FIELDS):
            q = center[f]
            inner = across[f, k] if tile == 0 else state[tile - 1, f, k + 1, body, :]
            outer = 0.0 if tile == tiles - 1 else state[tile + 1, f, k + 1, body, :]
            minus = pltpu.roll(jnp.where(lane_full == LANES - 1, inner, q), 1, 1)
            plus = pltpu.roll(jnp.where(lane_full == 0, outer, q), LANES - 1, 1)
            ahead = state[tile, f, k + 1, pl.ds(TOP + 1, theta_dev), :] - q
            behind = state[tile, f, k + 1, pl.ds(TOP - 1, theta_dev), :] - q
            up = state[tile, f, k + 2, body, :]
            down = state[tile, f, k, body, :]
            turn = ahead - behind
            turns.append(turn)
            out = q + (plus - minus) * radial + turn * around + (up - down) * axial
            out = out + spread_rate * ((plus + minus) + (up + down) - 4.0 * q)
            outs.append(out + theta_spread * (ahead + behind))
        whirl = turn_rate * center[1]
        outs[0] = outs[0] + whirl * center[1] - swirl * center[0] - cross * turns[1]
        outs[1] = outs[1] - whirl * center[0] - swirl * center[1] + cross * turns[0]
        outs[2] = outs[2] + (time_step * buoyancy) * center[3]
        for f in range(FIELDS):
            result[tile, f, k] = outs[f]

    stores = []

    def store(tile, first_plane, count):
        stores.append(
            pltpu.make_async_copy(
                result.at[tile, :, pl.ds(first_plane, count)],
                advanced.at[:, pl.ds(first_plane, count), :, pl.ds(tile * LANES, LANES)],
                store_sem.at[len(stores)],
            )
        )
        stores[-1].start()

    for tile in range(1, tiles):

        def far(k, carry):
            advance(tile, k)
            return carry

        lax.fori_loop(0, planes, far, 0)
        store(tile, 0, planes)

    sublane = lax.broadcasted_iota(jnp.int32, (half, LANES), 0)
    diagonal = (slot8 >= SPAN * sublane) & (slot8 < SPAN * sublane + SPAN)
    low_row = TOP - 1
    high_row = TOP + theta_dev
    is_near = lane < NEAR
    is_near_row = lane_row < NEAR

    def unpack(plane_list):
        updates = []
        for k in plane_list:
            tail = [
                state[0, 4, k + 1, TOP:middle, :],
                state[0, 4, k + 1, middle : middle + half, :],
                state[0, 4, k + 1, low_row : low_row + 1, :],
                state[0, 4, k + 1, high_row : high_row + 1, :],
            ]
            for f in range(4):
                got = recv2[owner(k, f)]
                turned = pltpu.roll(got, HALF, 1)
                rows = pltpu.roll(got, LANES - NEAR - QUARTER, 1, stride=SPAN, stride_axis=0)
                rows = jnp.sum(jnp.where(diagonal, rows, 0.0), axis=0, keepdims=True)
                parts = [
                    jnp.where(is_near, got, state[0, f, k + 1, TOP:middle, :]),
                    jnp.where(is_near, turned, state[0, f, k + 1, middle : middle + half, :]),
                    jnp.where(is_near_row, rows, state[0, f, k + 1, low_row : low_row + 1, :]),
                    jnp.where(
                        is_near_row,
                        pltpu.roll(rows, HALF, 1),
                        state[0, f, k + 1, high_row : high_row + 1, :],
                    ),
                ]
                updates.append((f, k, parts, turned, got))
                shift = (QUARTER * f - NEAR) % LANES
                other = (shift + HALF) % LANES
                part = (lane >= QUARTER * f) & (lane < QUARTER * (f + 1))
                part_row = (lane_row >= QUARTER * f) & (lane_row < QUARTER * (f + 1))
                tail[0] = jnp.where(part, pltpu.roll(got, shift, 1), tail[0])
                tail[1] = jnp.where(part, pltpu.roll(got, other, 1), tail[1])
                tail[2] = jnp.where(part_row, pltpu.roll(rows, shift, 1), tail[2])
                tail[3] = jnp.where(part_row, pltpu.roll(rows, other, 1), tail[3])
                if f == 0:
                    opposite = (pltpu.roll(got, HALF + 1, 1), pltpu.roll(got, 1, 1))
            updates.append((4, k, tail, *opposite))
        for f, k, parts, first, second in updates:
            state[0, f, k + 1, TOP:middle, :] = parts[0]
            state[0, f, k + 1, middle : middle + half, :] = parts[1]
            state[0, f, k + 1, low_row : low_row + 1, :] = parts[2]
            state[0, f, k + 1, high_row : high_row + 1, :] = parts[3]
            across[f, k, 0:half, :] = first
            across[f, k, half:, :] = second

    for copy in far_planes:
        copy.wait_send()

    def unpack_ghosts():
        updates = []
        for side, plane, edge in ((0, 0, 0), (1, planes + 1, slabs - 1)):
            inside = slab != edge
            tail0 = state[0, 4, plane, TOP:middle, :]
            tail1 = state[0, 4, plane, middle : middle + half, :]
            for f in range(4):
                got = ghost[side, f]
                part0 = jnp.where(is_near, got, state[0, f, plane, TOP:middle, :])
                part1 = jnp.where(
                    is_near,
                    pltpu.roll(got, HALF, 1),
                    state[0, f, plane, middle : middle + half, :],
                )
                updates.append((f, plane, inside, part0, part1))
                shift = (QUARTER * f - NEAR) % LANES
                part = (lane >= QUARTER * f) & (lane < QUARTER * (f + 1))
                tail0 = jnp.where(part, pltpu.roll(got, shift, 1), tail0)
                tail1 = jnp.where(part, pltpu.roll(got, (shift + HALF) % LANES, 1), tail1)
            updates.append((4, plane, inside, tail0, tail1))
        for f, plane, inside, part0, part1 in updates:
            state[0, f, plane, TOP:middle, :] = jnp.where(inside, part0, 0.0)
            state[0, f, plane, middle : middle + half, :] = jnp.where(inside, part1, 0.0)

    whole(recv2, 8, 1, 8).wait_recv()
    for f in range(4):
        for side, plane, neighbour in ((0, planes - 1, above), (1, 0, below)):
            pltpu.make_async_remote_copy(
                src_ref=recv2.at[owner(plane, f)],
                dst_ref=ghost.at[side, f],
                send_sem=send_sem.at[6 + side],
                recv_sem=recv_sem.at[6 + side],
                device_id={"ax": neighbour},
                device_id_type=MESH,
            ).start()
    unpack([0, planes - 1])
    whole(recv2, sectors - 8, 1, 1).wait_recv()

    def unpack_inner(i, carry):
        unpack([1 + i * WIDE + step for step in range(WIDE)])
        return carry

    lax.fori_loop(0, (planes - 2) // WIDE, unpack_inner, 0)

    def near(i, carry):
        for step in range(WIDE2):
            advance(0, 1 + i * WIDE2 + step)
        return carry

    lax.fori_loop(0, (planes - 2) // WIDE2, near, 0)
    store(0, 1, planes - 2)
    for side in range(2):
        whole(ghost.at[side], 4, 6 + side, 6 + side).wait_recv()
    unpack_ghosts()
    advance(0, 0)
    advance(0, planes - 1)
    store(0, 0, 1)
    store(0, planes - 1, 1)
    whole(send1, sectors, 0, 0).wait_send()
    whole(send2, sectors, 1, 1).wait_send()
    for side in range(2):
        whole(ghost.at[side], 4, 6 + side, 6 + side).wait_send()
    for copy in edges:
        copy.wait_send()
    for copy in stores:
        copy.wait()


def on_device(fields):
    sectors = lax.axis_size("az")
    slabs = lax.axis_size("ax")
    count, planes, theta_dev, radial = fields.shape
    half = theta_dev // 2
    tiles = radial // LANES
    forward, inverse = transform_tables(sectors, theta_dev)
    hbm = pl.BlockSpec(memory_space=pltpu.HBM)
    return pl.pallas_call(
        functools.partial(stencil_kernel, sectors, slabs),
        out_shape=jax.ShapeDtypeStruct(fields.shape, jnp.float32),
        in_specs=[hbm, hbm, hbm],
        out_specs=hbm,
        scratch_shapes=[
            pltpu.VMEM((tiles, count, planes + 2, theta_dev + 2 * TOP, LANES), jnp.float32),
            pltpu.VMEM((count, planes, theta_dev, LANES), jnp.float32),
            pltpu.VMEM((tiles, count, planes, theta_dev, LANES), jnp.float32),
            pltpu.VMEM(forward.shape, jnp.bfloat16),
            pltpu.VMEM(inverse.shape, jnp.bfloat16),
            pltpu.VMEM((sectors, half, LANES), jnp.float32),
            pltpu.VMEM((sectors, half, LANES), jnp.float32),
            pltpu.VMEM((sectors, half, LANES), jnp.float32),
            pltpu.VMEM((sectors, half, LANES), jnp.float32),
            pltpu.VMEM((sectors * half, LANES), jnp.float32),
            pltpu.VMEM((2, 4, half, LANES), jnp.float32),
            pltpu.VMEM((2, tiles, count, planes, LANES), jnp.float32),
            pltpu.VMEM((2, tiles, count, planes, LANES), jnp.float32),
            pltpu.SemaphoreType.DMA((tiles + 2,)),
            pltpu.SemaphoreType.DMA((tiles + 2,)),
            pltpu.SemaphoreType.DMA((8,)),
            pltpu.SemaphoreType.DMA((9,)),
        ],
        compiler_params=pltpu.CompilerParams(
            collective_id=0, has_side_effects=True, vmem_limit_bytes=48 << 20
        ),
        name="plume_section",
    )(
        pltpu.with_memory_space_constraint(fields, pltpu.HBM),
        pltpu.with_memory_space_constraint(jnp.asarray(forward), pltpu.HBM),
        pltpu.with_memory_space_constraint(jnp.asarray(inverse), pltpu.HBM),
    )


def solution(mesh):
    placed = (P(None, "ax", "az", None),)
    return jax.shard_map(
        on_device, mesh=mesh, in_specs=placed, out_specs=P(None, "ax", "az", None), check_vma=False
    )
```

```python
import functools

import jax
import jax.numpy as jnp
import ml_dtypes
import numpy as np
from jax import lax
from jax.experimental import pallas as pl
from jax.experimental.pallas import tpu as pltpu
from jax.sharding import PartitionSpec as P

NEAR = 40
FIELDS = 5
MODES = 128
LANES = 128
HALF = 64
QUARTER = 10
SPAN = 7
WIDE = 2
WIDE2 = 2
TOP = 8
MESH = pl.DeviceIdType.MESH

viscosity = 0.2
time_step = 0.1
buoyancy = 1.0


def split(table, pieces):
    out = []
    rest = table.astype(np.float32)
    for _ in range(pieces):
        piece = rest.astype(ml_dtypes.bfloat16)
        out.append(piece)
        rest = rest - piece.astype(np.float32)
    return np.stack(out)


def basis(theta, parity, total):
    mode = np.arange(parity, MODES, 2)
    angle = (theta[..., None] * mode % total) * (2.0 * np.pi / total)
    return np.concatenate([np.cos(angle), np.sin(angle)], axis=-1)


def transform_tables(sectors, theta_dev):
    total = sectors * theta_dev
    half = theta_dev // 2
    sector = np.arange(sectors // 2)[:, None] * theta_dev
    forward = []
    inverse = []
    for parity in range(2):
        mode = np.arange(parity, MODES, 2)
        weight = np.concatenate([np.where(mode == 0, 1.0, 2.0), np.full(MODES // 2, 2.0)]) / total
        into = []
        back = []
        for side in range(2):
            theta = (sector + side * half + np.arange(half)).reshape(-1)
            into.append((basis(theta, parity, total) * weight).T)
            edge = sector + (theta_dev if side else -1)
            theta = np.concatenate([theta, edge.reshape(-1)])
            back.append(basis(theta, parity, total))
        forward.append(split(np.concatenate(into, axis=0), 2))
        inverse.append(split(np.concatenate(back, axis=1), 3))
    return np.stack(forward), np.stack(inverse)


def stencil_kernel(
    sectors,
    slabs,
    fields,
    forward_hbm,
    inverse_hbm,
    advanced,
    state,
    across,
    result,
    forward,
    inverse,
    send1,
    recv1,
    send2,
    recv2,
    extra,
    ghost,
    edge_send,
    edge_recv,
    load_sem,
    store_sem,
    send_sem,
    recv_sem,
):
    me = lax.axis_index("az")
    slab = lax.axis_index("ax")
    planes = fields.shape[1]
    theta_dev = fields.shape[2]
    half = theta_dev // 2
    tiles = fields.shape[3] // LANES
    body = pl.ds(TOP, theta_dev)
    middle = TOP + half
    step_angle = 2.0 * np.pi / (sectors * theta_dev)

    loads = []
    for tile in range(tiles):
        loads.append(
            pltpu.make_async_copy(
                fields.at[:, :, :, pl.ds(tile * LANES, LANES)],
                state.at[tile, :, pl.ds(1, planes), body, :],
                load_sem.at[tile],
            )
        )
        loads[-1].start()
    load_forward = pltpu.make_async_copy(forward_hbm, forward, load_sem.at[tiles])
    load_forward.start()
    load_inverse = pltpu.make_async_copy(inverse_hbm, inverse, load_sem.at[tiles + 1])
    load_inverse.start()

    partner = (slab + slabs // 2) % slabs
    above = (slab + 1) % slabs
    below = (slab + slabs - 1) % slabs
    ahead = (me + 1) % sectors
    behind = (me + sectors - 1) % sectors
    own_x = me // 16
    own_y = me // 8 % 2
    own_z = me % 8

    own_group = own_z // 2
    own_plane = me // 8 * 2 + me % 2
    owns_edge = (own_plane == 0) | (own_plane == planes - 1)

    def owner(k, f):
        return k // 2 * 8 + 2 * f + k % 2

    around_x = [(own_x + step) % 4 * 16 for step in range(4)]
    around_y = [(own_y + step) % 2 * 8 for step in range(2)]
    around_z = [(own_z + step) % 8 for step in range(8)]

    def visit(call):
        for step_x in (2, 1, 3, 0):
            for step_z in (4, 0, 3, 1, 5, 7, 2, 6):
                for step_y in range(2):
                    call(around_x[step_x] + around_y[step_y] + around_z[step_z])

    barrier = pltpu.get_barrier_semaphore()

    def greet(peer):
        pl.semaphore_signal(
            barrier, inc=1, device_id={"az": peer, "ax": partner}, device_id_type=MESH
        )

    visit(greet)
    for neighbour in (above, below):
        pl.semaphore_signal(barrier, inc=1, device_id={"ax": neighbour}, device_id_type=MESH)
    for neighbour in (ahead, behind):
        pl.semaphore_signal(barrier, inc=1, device_id={"az": neighbour}, device_id_type=MESH)

    loads[0].wait()
    lane = lax.broadcasted_iota(jnp.int32, (half, LANES), 1)
    lane_row = lax.broadcasted_iota(jnp.int32, (1, LANES), 1)

    def pack(k, carry):
        tail0 = state[0, 4, k + 1, TOP:middle, :]
        tail1 = state[0, 4, k + 1, middle : middle + half, :]
        for f in range(4):
            shift = NEAR - QUARTER * f
            first = jnp.where(
                lane < NEAR, state[0, f, k + 1, TOP:middle, :], pltpu.roll(tail0, shift, 1)
            )
            second = jnp.where(
                lane < NEAR,
                state[0, f, k + 1, middle : middle + half, :],
                pltpu.roll(tail1, shift, 1),
            )
            send1[owner(k, f)] = jnp.where(lane < HALF, first, pltpu.roll(second, HALF, 1))
        return carry

    lax.fori_loop(0, planes, pack, 0)
    pl.semaphore_wait(barrier, sectors + 4)

    def exchange(source, target, index, arrival):
        def post(peer):
            pltpu.make_async_remote_copy(
                src_ref=source.at[peer],
                dst_ref=target.at[me],
                send_sem=send_sem.at[index],
                recv_sem=recv_sem.at[arrival],
                device_id={"az": peer, "ax": partner},
                device_id_type=MESH,
            ).start()

        visit(post)

    def whole(buffer, count, index, arrival):
        return pltpu.make_async_remote_copy(
            src_ref=buffer.at[pl.ds(0, count)],
            dst_ref=buffer.at[pl.ds(0, count)],
            send_sem=send_sem.at[index],
            recv_sem=recv_sem.at[arrival],
            device_id={"az": me, "ax": partner},
            device_id_type=MESH,
        )

    exchange(send1, recv1, 0, 0)

    def plane_copy(first_tile, count, source, target, neighbour, index):
        return pltpu.make_async_remote_copy(
            src_ref=state.at[pl.ds(first_tile, count), :, source, body, :],
            dst_ref=state.at[pl.ds(first_tile, count), :, target, body, :],
            send_sem=send_sem.at[index],
            recv_sem=recv_sem.at[index],
            device_id={"ax": neighbour},
            device_id_type=MESH,
        )

    for load in loads[1:]:
        load.wait()
    far_planes = [
        plane_copy(0, tiles, planes, 0, above, 2),
        plane_copy(0, tiles, 1, planes + 1, below, 3),
    ]
    for copy in far_planes:
        copy.start()

    def collect(i, carry):
        tile = i // FIELDS
        f = i % FIELDS
        for k in range(planes):
            edge_send[0, tile, f, k : k + 1, :] = state[tile, f, k + 1, TOP : TOP + 1, :]
            edge_send[1, tile, f, k : k + 1, :] = state[
                tile, f, k + 1, TOP + theta_dev - 1 : TOP + theta_dev, :
            ]
        return carry

    lax.fori_loop(0, tiles * FIELDS, collect, 0)
    edges = []
    for side, peer in ((0, behind), (1, ahead)):
        edges.append(
            pltpu.make_async_remote_copy(
                src_ref=edge_send.at[side],
                dst_ref=edge_recv.at[side],
                send_sem=send_sem.at[4 + side],
                recv_sem=recv_sem.at[4 + side],
                device_id={"az": peer},
                device_id_type=MESH,
            )
        )
        edges[-1].start()

    load_forward.wait()
    load_inverse.wait()
    whole(recv1, sectors, 0, 0).wait_recv()
    dot = functools.partial(jnp.dot, preferred_element_type=jnp.float32)
    pairs = sectors // 2
    row = lax.broadcasted_iota(jnp.int32, (MODES, LANES), 0)
    column = lax.broadcasted_iota(jnp.int32, (MODES, LANES), 1)
    slot = jnp.where(column < HALF, column, column - HALF)
    group = own_group
    cycle = jnp.where(slot < NEAR, slot, slot - NEAR + QUARTER * group)
    cutoff = jnp.floor((355 * (2 * cycle + 1)).astype(jnp.float32) / 226.0 + 0.001)
    cutoff = jnp.minimum(cutoff, MODES - 1.0)
    vector_sign = jnp.where(group < 2, -1.0, 1.0)
    smooth = []
    for parity in range(2):
        near_half = recv1[0:pairs].reshape(pairs * half, LANES)
        far_half = recv1[pairs:].reshape(pairs * half, LANES)
        values = near_half - far_half if parity else near_half + far_half
        high = values.astype(jnp.bfloat16)
        low = (values - high.astype(jnp.float32)).astype(jnp.bfloat16)
        both = dot(forward[parity, 0], jnp.concatenate([high, low], axis=1))
        spectra = both[:, :LANES] + (both[:, LANES:] + dot(forward[parity, 1], high))
        spectra = jnp.where(column < HALF, spectra[:MODES], spectra[MODES:])
        spectra = spectra + pltpu.roll(spectra, HALF, 1)
        mode = 2 * jnp.where(row < MODES // 2, row, row - MODES // 2) + parity
        spectra = jnp.where(mode.astype(jnp.float32) <= cutoff, spectra, 0.0)
        sign = -1.0 if parity else 1.0
        spectra = jnp.where(
            slot == HALF - 1,
            (sign * vector_sign) * pltpu.roll(spectra, HALF - 1, 1),
            jnp.where(slot == HALF - 2, sign * pltpu.roll(spectra, HALF - 2 - NEAR, 1), spectra),
        )
        spectra = jnp.concatenate(
            [jnp.where(column < HALF, spectra, 0.0), jnp.where(column < HALF, 0.0, spectra)],
            axis=0,
        )
        high = spectra.astype(jnp.bfloat16)
        rest = spectra - high.astype(jnp.float32)
        medium = rest.astype(jnp.bfloat16)
        low = (rest - medium.astype(jnp.float32)).astype(jnp.bfloat16)
        wide = jnp.concatenate([high, medium], axis=1)
        first = dot(inverse[parity, 0], wide)
        second = dot(inverse[parity, 1], wide)
        third = dot(inverse[parity, 0], low) + dot(inverse[parity, 2], high)
        third = third + second[:, LANES:]
        smooth.append(first[:, :LANES] + (first[:, LANES:] + second[:, :LANES] + third))
    for side in range(2):
        value = smooth[0] - smooth[1] if side else smooth[0] + smooth[1]
        send2[side * pairs : (side + 1) * pairs] = value[: pairs * half].reshape(
            pairs, half, LANES
        )
        for i in range(half):
            first_row = i * sectors + side * pairs
            extra[first_row : first_row + pairs, :] = pltpu.roll(
                value[pairs * half :], (NEAR + QUARTER - SPAN * i) % LANES, 1
            )

    slot8 = jnp.where(lane < HALF, lane, lane - HALF)
    spare = (slot8 >= NEAR + QUARTER) & (slot8 < NEAR + QUARTER + SPAN)

    def edge_lanes(i, carry):
        for d in range(8):
            turned = extra[pl.ds(i * 8 + d, half, stride=sectors), :]
            send2[i * 8 + d] = jnp.where(spare, turned, send2[i * 8 + d])
        return carry

    lax.fori_loop(0, sectors // 8, edge_lanes, 0)
    exchange(send2, recv2, 1, jnp.where(owns_edge, 8, 1))

    for copy in edges + far_planes:
        copy.wait_recv()

    def spread(i, carry):
        tile = i // FIELDS
        f = i % FIELDS
        for k in range(planes):
            state[tile, f, k + 1, TOP - 1 : TOP, :] = edge_recv[1, tile, f, k : k + 1, :]
            state[tile, f, k + 1, TOP + theta_dev : TOP + theta_dev + 1, :] = edge_recv[
                0, tile, f, k : k + 1, :
            ]
        return carry

    lax.fori_loop(0, tiles * FIELDS, spread, 0)

    def close(first_tile, last_tile):
        nothing = jnp.zeros((theta_dev, LANES), jnp.float32)
        for plane, edge in ((0, 0), (planes + 1, slabs - 1)):

            @pl.when(slab == edge)
            def _():
                for tile in range(first_tile, last_tile):
                    for f in range(FIELDS):
                        state[tile, f, plane, body, :] = nothing

    close(1, tiles)
    lane_full = lax.broadcasted_iota(jnp.int32, (theta_dev, LANES), 1)

    def advance(tile, k):
        radius = (lane_row + tile * LANES).astype(jnp.float32) + 0.5
        inverse_radius = 1.0 / radius
        inverse_square = 1.0 / (radius * radius)
        spread_rate = time_step * viscosity
        radial_base = (0.5 * spread_rate) * inverse_radius
        theta_rate = (-time_step / (2.0 * step_angle)) * inverse_radius
        theta_spread = (spread_rate / (step_angle * step_angle)) * inverse_square
        turn_rate = time_step * inverse_radius
        swirl = spread_rate * inverse_square
        cross = (spread_rate / step_angle) * inverse_square
        center = [state[tile, f, k + 1, body, :] for f in range(FIELDS)]
        radial = radial_base - (0.5 * time_step) * center[0]
        around = theta_rate * center[1]
        axial = (-0.5 * time_step) * center[2]
        outs = []
        turns = []
        for f in range(FIELDS):
            q = center[f]
            inner = across[f, k] if tile == 0 else state[tile - 1, f, k + 1, body, :]
            outer = 0.0 if tile == tiles - 1 else state[tile + 1, f, k + 1, body, :]
            minus = pltpu.roll(jnp.where(lane_full == LANES - 1, inner, q), 1, 1)
            plus = pltpu.roll(jnp.where(lane_full == 0, outer, q), LANES - 1, 1)
            ahead = state[tile, f, k + 1, pl.ds(TOP + 1, theta_dev), :] - q
            behind = state[tile, f, k + 1, pl.ds(TOP - 1, theta_dev), :] - q
            up = state[tile, f, k + 2, body, :]
            down = state[tile, f, k, body, :]
            turn = ahead - behind
            turns.append(turn)
            out = q + (plus - minus) * radial + turn * around + (up - down) * axial
            out = out + spread_rate * ((plus + minus) + (up + down) - 4.0 * q)
            outs.append(out + theta_spread * (ahead + behind))
        whirl = turn_rate * center[1]
        outs[0] = outs[0] + whirl * center[1] - swirl * center[0] - cross * turns[1]
        outs[1] = outs[1] - whirl * center[0] - swirl * center[1] + cross * turns[0]
        outs[2] = outs[2] + (time_step * buoyancy) * center[3]
        for f in range(FIELDS):
            result[tile, f, k] = outs[f]

    stores = []

    def store(tile, first_plane, count):
        stores.append(
            pltpu.make_async_copy(
                result.at[tile, :, pl.ds(first_plane, count)],
                advanced.at[:, pl.ds(first_plane, count), :, pl.ds(tile * LANES, LANES)],
                store_sem.at[len(stores)],
            )
        )
        stores[-1].start()

    for tile in range(1, tiles):

        def far(k, carry):
            advance(tile, 2 * k + 0)
            advance(tile, 2 * k + 1)
            return carry

        lax.fori_loop(0, planes // 2, far, 0)
        store(tile, 0, planes)

    sublane = lax.broadcasted_iota(jnp.int32, (half, LANES), 0)
    diagonal = (slot8 >= SPAN * sublane) & (slot8 < SPAN * sublane + SPAN)
    low_row = TOP - 1
    high_row = TOP + theta_dev
    is_near = lane < NEAR
    is_near_row = lane_row < NEAR

    def unpack(plane_list):
        updates = []
        for k in plane_list:
            tail = [
                state[0, 4, k + 1, TOP:middle, :],
                state[0, 4, k + 1, middle : middle + half, :],
                state[0, 4, k + 1, low_row : low_row + 1, :],
                state[0, 4, k + 1, high_row : high_row + 1, :],
            ]
            for f in range(4):
                got = recv2[owner(k, f)]
                turned = pltpu.roll(got, HALF, 1)
                rows = pltpu.roll(got, LANES - NEAR - QUARTER, 1, stride=SPAN, stride_axis=0)
                rows = jnp.sum(jnp.where(diagonal, rows, 0.0), axis=0, keepdims=True)
                parts = [
                    jnp.where(is_near, got, state[0, f, k + 1, TOP:middle, :]),
                    jnp.where(is_near, turned, state[0, f, k + 1, middle : middle + half, :]),
                    jnp.where(is_near_row, rows, state[0, f, k + 1, low_row : low_row + 1, :]),
                    jnp.where(
                        is_near_row,
                        pltpu.roll(rows, HALF, 1),
                        state[0, f, k + 1, high_row : high_row + 1, :],
                    ),
                ]
                updates.append((f, k, parts, turned, got))
                shift = (QUARTER * f - NEAR) % LANES
                other = (shift + HALF) % LANES
                part = (lane >= QUARTER * f) & (lane < QUARTER * (f + 1))
                part_row = (lane_row >= QUARTER * f) & (lane_row < QUARTER * (f + 1))
                tail[0] = jnp.where(part, pltpu.roll(got, shift, 1), tail[0])
                tail[1] = jnp.where(part, pltpu.roll(got, other, 1), tail[1])
                tail[2] = jnp.where(part_row, pltpu.roll(rows, shift, 1), tail[2])
                tail[3] = jnp.where(part_row, pltpu.roll(rows, other, 1), tail[3])
                if f == 0:
                    opposite = (pltpu.roll(got, HALF + 1, 1), pltpu.roll(got, 1, 1))
            updates.append((4, k, tail, *opposite))
        for f, k, parts, first, second in updates:
            state[0, f, k + 1, TOP:middle, :] = parts[0]
            state[0, f, k + 1, middle : middle + half, :] = parts[1]
            state[0, f, k + 1, low_row : low_row + 1, :] = parts[2]
            state[0, f, k + 1, high_row : high_row + 1, :] = parts[3]
            across[f, k, 0:half, :] = first
            across[f, k, half:, :] = second

    for copy in far_planes:
        copy.wait_send()

    def unpack_ghosts():
        updates = []
        for side, plane, edge in ((0, 0, 0), (1, planes + 1, slabs - 1)):
            inside = slab != edge
            tail0 = state[0, 4, plane, TOP:middle, :]
            tail1 = state[0, 4, plane, middle : middle + half, :]
            for f in range(4):
                got = ghost[side, f]
                part0 = jnp.where(is_near, got, state[0, f, plane, TOP:middle, :])
                part1 = jnp.where(
                    is_near,
                    pltpu.roll(got, HALF, 1),
                    state[0, f, plane, middle : middle + half, :],
                )
                updates.append((f, plane, inside, part0, part1))
                shift = (QUARTER * f - NEAR) % LANES
                part = (lane >= QUARTER * f) & (lane < QUARTER * (f + 1))
                tail0 = jnp.where(part, pltpu.roll(got, shift, 1), tail0)
                tail1 = jnp.where(part, pltpu.roll(got, (shift + HALF) % LANES, 1), tail1)
            updates.append((4, plane, inside, tail0, tail1))
        for f, plane, inside, part0, part1 in updates:
            state[0, f, plane, TOP:middle, :] = jnp.where(inside, part0, 0.0)
            state[0, f, plane, middle : middle + half, :] = jnp.where(inside, part1, 0.0)

    whole(recv2, 8, 1, 8).wait_recv()
    for f in range(4):
        for side, plane, neighbour in ((0, planes - 1, above), (1, 0, below)):
            pltpu.make_async_remote_copy(
                src_ref=recv2.at[owner(plane, f)],
                dst_ref=ghost.at[side, f],
                send_sem=send_sem.at[6 + side],
                recv_sem=recv_sem.at[6 + side],
                device_id={"ax": neighbour},
                device_id_type=MESH,
            ).start()
    unpack([0, planes - 1])
    whole(recv2, sectors - 8, 1, 1).wait_recv()

    def unpack_inner(i, carry):
        unpack([1 + i * WIDE + step for step in range(WIDE)])
        return carry

    lax.fori_loop(0, (planes - 2) // WIDE, unpack_inner, 0)

    def near(i, carry):
        for step in range(WIDE2):
            advance(0, 1 + i * WIDE2 + step)
        return carry

    lax.fori_loop(0, (planes - 2) // WIDE2, near, 0)
    store(0, 1, planes - 2)
    for side in range(2):
        whole(ghost.at[side], 4, 6 + side, 6 + side).wait_recv()
    unpack_ghosts()
    advance(0, 0)
    advance(0, planes - 1)
    store(0, 0, 1)
    store(0, planes - 1, 1)
    whole(send1, sectors, 0, 0).wait_send()
    whole(send2, sectors, 1, 1).wait_send()
    for side in range(2):
        whole(ghost.at[side], 4, 6 + side, 6 + side).wait_send()
    for copy in edges:
        copy.wait_send()
    for copy in stores:
        copy.wait()


def on_device(fields):
    sectors = lax.axis_size("az")
    slabs = lax.axis_size("ax")
    count, planes, theta_dev, radial = fields.shape
    half = theta_dev // 2
    tiles = radial // LANES
    forward, inverse = transform_tables(sectors, theta_dev)
    hbm = pl.BlockSpec(memory_space=pltpu.HBM)
    return pl.pallas_call(
        functools.partial(stencil_kernel, sectors, slabs),
        out_shape=jax.ShapeDtypeStruct(fields.shape, jnp.float32),
        in_specs=[hbm, hbm, hbm],
        out_specs=hbm,
        scratch_shapes=[
            pltpu.VMEM((tiles, count, planes + 2, theta_dev + 2 * TOP, LANES), jnp.float32),
            pltpu.VMEM((count, planes, theta_dev, LANES), jnp.float32),
            pltpu.VMEM((tiles, count, planes, theta_dev, LANES), jnp.float32),
            pltpu.VMEM(forward.shape, jnp.bfloat16),
            pltpu.VMEM(inverse.shape, jnp.bfloat16),
            pltpu.VMEM((sectors, half, LANES), jnp.float32),
            pltpu.VMEM((sectors, half, LANES), jnp.float32),
            pltpu.VMEM((sectors, half, LANES), jnp.float32),
            pltpu.VMEM((sectors, half, LANES), jnp.float32),
            pltpu.VMEM((sectors * half, LANES), jnp.float32),
            pltpu.VMEM((2, 4, half, LANES), jnp.float32),
            pltpu.VMEM((2, tiles, count, planes, LANES), jnp.float32),
            pltpu.VMEM((2, tiles, count, planes, LANES), jnp.float32),
            pltpu.SemaphoreType.DMA((tiles + 2,)),
            pltpu.SemaphoreType.DMA((tiles + 2,)),
            pltpu.SemaphoreType.DMA((8,)),
            pltpu.SemaphoreType.DMA((9,)),
        ],
        compiler_params=pltpu.CompilerParams(
            collective_id=0, has_side_effects=True, vmem_limit_bytes=48 << 20
        ),
        name="plume_section",
    )(
        pltpu.with_memory_space_constraint(fields, pltpu.HBM),
        pltpu.with_memory_space_constraint(jnp.asarray(forward), pltpu.HBM),
        pltpu.with_memory_space_constraint(jnp.asarray(inverse), pltpu.HBM),
    )


def solution(mesh):
    placed = (P(None, "ax", "az", None),)
    return jax.shard_map(
        on_device, mesh=mesh, in_specs=placed, out_specs=P(None, "ax", "az", None), check_vma=False
    )
```
